32 devices in a mesh: parts: 2 (over x), seq: 8 (over z, y), head: 2 (over core).
Axes of the slice: x: 2, y: 2, z: 4, core: 2. Of those that a mesh axis runs over, the one named last changes fastest.
Arguments:
- latents: bfloat16 [8192, 2112], P(('parts', 'seq', 'head')), parts along dimension 0, may hold values from -400 to 400
- q_gain: float32 [1536], replicated, may hold values from 0.25 to 1.75
- kv_gain: float32 [512], replicated, may hold values from 0.25 to 1.75
- q_weight: bfloat16 [2, 1536, 32, 192], P('head', None, 'seq'), may hold values from -0.15625 to 0.15625
- kv_weight: bfloat16 [2, 512, 32, 256], P('head', None, 'seq'), may hold values from -0.25 to 0.25
- lengths: int32 [16, 8], P('parts'), parts along dimension 0, may hold values from 0 to 512, as said below
Outputs:
- attended: bfloat16 [8192, 8192], P(('parts', 'seq'), 'head'), parts along dimension 0
The draws below stay inside these ranges and needn't reach their ends.
There are 2 independent parts, one for each index of `parts`. The reference program is written for one: setup_inputs(seed, part) draws one part's arguments, and reference() takes and returns one part's arrays. A program takes and returns all parts, laid end to end along the dimension named above; an argument that names none is the same for every part. Nothing has to cross between parts.
Inputs may be any that keep to these rules, and one draw needn't show every extreme that they name: Row g lists the lengths of the sequences packed in order in group g: they sum to 512, each is a multiple of 64, the nonzero ones come first. Some group holds a single sequence of 512 tokens; the group after it holds two sequences of 256 tokens, and the group 8 / 2 after that one holds 8 sequences of 64 tokens.
All inputs are finite; a program needn't handle non-finite values.
Results may differ from the reference program's by a relative error of at most 0.011.
Values may be sent and summed in bfloat16 or wider, within the bound.
A program may use at most 128 MiB of HBM per device.

```python
import jax
import jax.numpy as jnp
from jax import lax

Q_LAT = 1536
KV_LAT = 512
ROPE = 64
NOPE = 128
VD = 128
H = 64
SLOTS = 8
TOK_DEV = 512
GROUPS = 8
HSH = 2
TOKENS = 4096


def draw_latents(key, part):
    key_base = jax.random.fold_in(key, 0)
    width_all = Q_LAT + KV_LAT + ROPE
    base_draw = jax.random.truncated_normal(key_base, -5.0, 5.0, (TOKENS, width_all), jnp.float32)
    return jnp.clip(base_draw, -400.0, 400.0).astype(jnp.bfloat16)


def draw_lengths(key, part):
    key_rate, key_bits, key_single = jax.random.split(key, 3)
    cut_rate = jax.random.randint(key_rate, (GROUPS, 1), 0, SLOTS)
    cut_bits = jax.random.randint(key_bits, (GROUPS, SLOTS - 1), 0, SLOTS) < cut_rate
    single_group = jax.random.randint(key_single, (), 0, GROUPS)
    cut_bits = cut_bits & (jnp.arange(GROUPS)[:, None] != single_group)
    ones_col = jnp.ones((GROUPS, 1), jnp.int32)
    edge_marks = jnp.concatenate([ones_col, cut_bits.astype(jnp.int32), ones_col], axis=1)
    edge_rank = jnp.cumsum(edge_marks, axis=1)
    slot_ids = jnp.arange(SLOTS + 1)
    hits = (edge_marks[:, :, None] == 1) & (edge_rank[:, :, None] == slot_ids[None, None, :] + 1)
    edge_where = jnp.sum(jnp.where(hits, slot_ids[None, :, None], 0), axis=1)
    edge_count = edge_rank[:, -1]
    order_ids = jnp.arange(SLOTS)
    valid = order_ids[None, :] + 1 < edge_count[:, None]
    span_sizes = edge_where[:, 1:] - edge_where[:, :-1]
    drawn = (jnp.where(valid, span_sizes, 0) * (TOK_DEV // SLOTS)).astype(jnp.int32)
    heavy_group = (single_group + 1) % GROUPS
    light_group = (heavy_group + GROUPS // 2) % GROUPS
    heavy_row = jnp.where(order_ids < 2, TOK_DEV // 2, 0).astype(jnp.int32)
    light_row = jnp.full((SLOTS,), TOK_DEV // SLOTS, jnp.int32)
    group_ids = jnp.arange(GROUPS)[:, None]
    drawn = jnp.where(group_ids == heavy_group, heavy_row[None, :], drawn)
    drawn = jnp.where(group_ids == light_group, light_row[None, :], drawn)
    return drawn.astype(jnp.int32)


def block_levels(key, shape, cuts, low, high):
    factor_of, own = 1.0, jax.random.fold_in(key, 6)
    for axis_at, blocks in cuts:
        steps = jnp.exp(jax.random.uniform(jax.random.fold_in(own, axis_at), (blocks,), jnp.float32, low / len(cuts), high / len(cuts)))
        factor_of = factor_of * jnp.repeat(steps, shape[axis_at] // blocks).reshape([-1 if axis == axis_at else 1 for axis in range(len(shape))])
    return factor_of


def centred(key, shape, width, most, cuts=(), kind=jnp.bfloat16):
    loudness = block_levels(key, shape, cuts, -0.22, 0.18) if cuts else 1.0
    values = jax.random.normal(key, shape, jnp.float32) * width * loudness
    return jnp.minimum(jnp.maximum(values, -most), most).astype(kind)


def setup_inputs(seed: int = 0, part: int = 0) -> dict:
    key_list = jax.random.split(jax.random.key(seed), 7)
    own_keys = jax.random.split(jax.random.fold_in(key_list[6], part), 7)
    latents = draw_latents(jax.random.fold_in(jax.random.fold_in(key_list[6], part), 71), part)
    q_gain = jnp.clip(1.0 + 0.15 * jax.random.normal(key_list[1], (Q_LAT,), jnp.float32), 0.25, 1.75)
    kv_gain = jnp.clip(1.0 + 0.15 * jax.random.normal(key_list[2], (KV_LAT,), jnp.float32), 0.25, 1.75)
    q_weight = centred(key_list[3], (HSH, Q_LAT, H // HSH, NOPE + ROPE), Q_LAT ** -0.5, 0.15625, ((0, 2), (2, 8)))
    kv_weight = centred(key_list[4], (HSH, KV_LAT, H // HSH, NOPE + VD), KV_LAT ** -0.5, 0.25, ((0, 2), (2, 8)))
    lengths = draw_lengths(jax.random.fold_in(jax.random.fold_in(key_list[6], part), 71), part)
    return {"latents": latents, "q_gain": q_gain, "kv_gain": kv_gain, "q_weight": q_weight, "kv_weight": kv_weight, "lengths": lengths}


epsilon = 1e-06

def rotary(values, positions):
    half_width = values.shape[-1] // 2
    freq_table = jnp.exp(jnp.arange(half_width, dtype=jnp.float32) * (-2.0 * jnp.log(10000.0) / values.shape[-1]))
    angles = positions.astype(jnp.float32)[:, None] * freq_table[None, :]
    if values.ndim == 3:
        angles = angles[:, None, :]
    cosine = jnp.cos(angles)
    sine_part = jnp.sin(angles)
    first_half = values[..., :half_width]
    second_half = values[..., half_width:]
    return jnp.concatenate([first_half * cosine - second_half * sine_part, second_half * cosine + first_half * sine_part], axis=-1)

def normalize(part_values, gain_vec):
    squares = lax.optimization_barrier(jnp.mean(part_values * part_values, axis=-1, keepdims=True))
    return (part_values * lax.rsqrt(squares + epsilon) * gain_vec).astype(jnp.bfloat16)

def seq_starts(length_row, token_count):
    seq_ends = jnp.cumsum(length_row).astype(jnp.int32)
    begins = (seq_ends - length_row).astype(jnp.int32)
    token_ids = jnp.arange(token_count, dtype=jnp.int32)
    inside = (token_ids[:, None] >= begins[None, :]) & (token_ids[:, None] < seq_ends[None, :])
    return lax.optimization_barrier(jnp.sum(jnp.where(inside, begins[None, :], 0), axis=1)).astype(jnp.int32)

def prepare(block_rows, q_gain, kv_gain, positions):
    q_width = q_gain.shape[0]
    kv_width = kv_gain.shape[0]
    q_part = block_rows[:, :q_width].astype(jnp.float32)
    kv_part = block_rows[:, q_width:q_width + kv_width].astype(jnp.float32)
    rope_part = block_rows[:, q_width + kv_width:].astype(jnp.float32)
    return (normalize(q_part, q_gain), normalize(kv_part, kv_gain), rotary(rope_part, positions).astype(jnp.bfloat16))

def dense_attention(queries, key_values, rope_keys, begins):
    token_count = queries.shape[0]
    rope_width = rope_keys.shape[1]
    nope_width = queries.shape[2] - rope_width
    score_scale = queries.shape[2] ** (-0.5)
    query_full = queries.astype(jnp.float32)
    pair_full = key_values.astype(jnp.float32)
    scores = jnp.einsum('qhd,khd->hqk', query_full[:, :, :nope_width], pair_full[:, :, :nope_width])
    scores = scores + jnp.einsum('qhd,kd->hqk', query_full[:, :, nope_width:], rope_keys.astype(jnp.float32))
    token_ids = jnp.arange(token_count, dtype=jnp.int32)
    allowed = (begins[:, None] <= token_ids[None, :]) & (token_ids[None, :] <= token_ids[:, None])
    scores = jnp.where(allowed[None], scores * score_scale, -jnp.inf)
    maxima = lax.optimization_barrier(jnp.max(scores, axis=-1, keepdims=True))
    exp_terms = jnp.exp(scores - maxima)
    totals = lax.optimization_barrier(jnp.sum(exp_terms, axis=-1))
    softmax_num = lax.optimization_barrier(exp_terms.astype(jnp.bfloat16)).astype(jnp.float32)
    mixed_out = jnp.einsum('hqk,khd->qhd', softmax_num, pair_full[:, :, nope_width:])
    return (mixed_out / totals.T[:, :, None]).astype(jnp.bfloat16)

def reference(latents, q_gain, kv_gain, q_weight, kv_weight, lengths):
    shard_count = q_weight.shape[0]
    per_shard = q_weight.shape[2]
    head_total = shard_count * per_shard
    query_table = jnp.transpose(q_weight, (1, 0, 2, 3)).reshape(q_weight.shape[1], head_total, q_weight.shape[3]).astype(jnp.float32)
    pair_table = jnp.transpose(kv_weight, (1, 0, 2, 3)).reshape(kv_weight.shape[1], head_total, kv_weight.shape[3]).astype(jnp.float32)
    group_count = lengths.shape[0]
    token_count = latents.shape[0] // group_count
    group_blocks = latents.reshape(group_count, token_count, latents.shape[1])

    def one_group(group_args):
        block_rows, length_row = group_args
        begins = seq_starts(length_row, token_count)
        positions = jnp.arange(token_count, dtype=jnp.int32) - begins
        q_normed, kv_normed, rope_keys = prepare(block_rows, q_gain, kv_gain, positions)
        projected = jnp.einsum('tc,chd->thd', q_normed.astype(jnp.float32), query_table)
        nope_width = projected.shape[2] - rope_keys.shape[1]
        queries = jnp.concatenate([projected[:, :, :nope_width], rotary(projected[:, :, nope_width:], positions)], axis=-1).astype(jnp.bfloat16)
        key_values = jnp.einsum('tc,chd->thd', kv_normed.astype(jnp.float32), pair_table).astype(jnp.bfloat16)
        mixed_out = dense_attention(queries, key_values, rope_keys, begins)
        return mixed_out.reshape(token_count, -1)
    return lax.map(one_group, (group_blocks, lengths)).reshape(latents.shape[0], -1)
```

```python
import functools
import math

import jax
import jax.numpy as jnp
import numpy as np
from jax import lax
from jax.experimental import pallas as pl
from jax.experimental.pallas import tpu as pltpu
from jax.sharding import PartitionSpec as P

EPSILON = 1e-06
MASKED = -1e30
CHUNKS = 3
MESH = pl.DeviceIdType.MESH


def kernel(
    n_line, nh, q_width, kv_width, rope, nope, vd, tokens, slots,
    lengths, freqs, q_gain, kv_gain, latents, wq, wkv,
    out,
    wq_buf, wkv_buf, lat, qn, kvn, cosine, sine, kr, bias, q_s, k_s, v_s, obuf,
    own_sem, lat_send, lat_recv, line_send, line_recv, x_send, x_recv, out_local, out_send, out_recv,
):
    part = lax.axis_index("parts")
    seq = lax.axis_index("seq")
    core = lax.axis_index("head")
    half = lax.rem(part, 2)
    pos = seq // 2
    parity = lax.rem(seq, 2)
    pair = {"seq": seq + 1 - 2 * parity}
    sibling = {"head": 1 - core}
    across = {"parts": part + 1 - 2 * half}
    left = {"seq": jnp.maximum(seq - 2, parity)}
    right = {"seq": jnp.minimum(seq + 2, 2 * (n_line - 1) + parity)}
    has_left = pos > 0
    has_right = pos < n_line - 1
    half_tokens = tokens // 2
    q_rows = q_width // 4
    kv_rows = kv_width // 2

    def piece(q_ref, kv_ref, side, chunk):
        if chunk < 2:
            start = pl.multiple_of(side * (2 * q_rows) + chunk * q_rows, q_rows)
            return q_ref.at[pl.ds(start, q_rows), :]
        return kv_ref.at[pl.ds(pl.multiple_of(side * kv_rows, kv_rows), kv_rows), :]

    def slot(block, side, chunk):
        return piece(wq_buf.at[block], wkv_buf.at[block], side, chunk)

    def line_copy(block, chunk, direction):
        return pltpu.make_async_remote_copy(
            src_ref=slot(block, half, chunk), dst_ref=slot(block, half, chunk),
            send_sem=line_send.at[direction, block, chunk], recv_sem=line_recv.at[block, chunk],
            device_id=(left, right)[direction], device_id_type=MESH,
        )

    def own_line_copy(chunk, direction):
        return pltpu.make_async_remote_copy(
            src_ref=piece(wq, wkv, half, chunk), dst_ref=slot(pos, half, chunk),
            send_sem=line_send.at[direction, pos, chunk], recv_sem=line_recv.at[pos, chunk],
            device_id=(left, right)[direction], device_id_type=MESH,
        )

    def x_copy(block, chunk, side):
        return pltpu.make_async_remote_copy(
            src_ref=slot(block, side, chunk), dst_ref=slot(block, side, chunk),
            send_sem=x_send.at[block, chunk], recv_sem=x_recv.at[block, chunk],
            device_id=across, device_id_type=MESH,
        )

    def lat_copy(source, group, owner, target, index):
        return pltpu.make_async_remote_copy(
            src_ref=source, dst_ref=lat.at[group, owner],
            send_sem=lat_send.at[index], recv_sem=lat_recv.at[index],
            device_id=target, device_id_type=MESH,
        )

    barrier = pltpu.get_barrier_semaphore()
    for target in (pair, sibling, across):
        pl.semaphore_signal(barrier, inc=1, device_id=target, device_id_type=MESH)

    @pl.when(has_left)
    def _():
        pl.semaphore_signal(barrier, inc=1, device_id=left, device_id_type=MESH)

    @pl.when(has_right)
    def _():
        pl.semaphore_signal(barrier, inc=1, device_id=right, device_id_type=MESH)

    own_lat = pltpu.make_async_copy(latents, lat.at[0, core], own_sem.at[0])
    own_wq = pltpu.make_async_copy(wq, wq_buf.at[pos], own_sem.at[1])
    own_wkv = pltpu.make_async_copy(wkv, wkv_buf.at[pos], own_sem.at[2])
    own_lat.start()
    own_wq.start()
    own_wkv.start()

    pl.semaphore_wait(barrier, 3 + has_left.astype(jnp.int32) + has_right.astype(jnp.int32))

    lat_copy(latents, 0, core, sibling, 0).start()
    lat_copy(latents, 1, core, pair, 1).start()

    @pl.when(has_left)
    def _():
        for chunk in range(CHUNKS):
            own_line_copy(chunk, 0).start()

    @pl.when(has_right)
    def _():
        for chunk in range(CHUNKS):
            own_line_copy(chunk, 1).start()

    def forward(distance, chunk):
        @pl.when(pos - distance >= 0)
        def _():
            block = jnp.maximum(pos - distance, 0)
            line_copy(block, chunk, 1).wait_recv()

            @pl.when(has_right)
            def _():
                line_copy(block, chunk, 1).start()

            x_copy(block, chunk, half).start()

        @pl.when(pos + distance < n_line)
        def _():
            block = jnp.minimum(pos + distance, n_line - 1)
            line_copy(block, chunk, 0).wait_recv()

            @pl.when(has_left)
            def _():
                line_copy(block, chunk, 0).start()

            x_copy(block, chunk, half).start()

    unit = tokens // slots

    def tables(group):
        index = jnp.where(group == 0, seq, seq + 1 - 2 * parity)
        spans = []
        begin = jnp.int32(0)
        for i in range(slots):
            end = begin + lengths[index, i]
            spans.append((begin, end))
            begin = end

        def begins_of(ids):
            found = jnp.zeros_like(ids)
            for low, high in spans:
                found = jnp.where((ids >= low) & (ids < high), low, found)
            return found

        freq = freqs[...]
        fine = lax.broadcasted_iota(jnp.int32, (unit, 128), 0).astype(jnp.float32) * freq
        fine_cos, fine_sin = jnp.cos(fine), jnp.sin(fine)
        coarse_ids = lax.broadcasted_iota(jnp.int32, (slots, 128), 0) * unit
        coarse = (coarse_ids - begins_of(coarse_ids)).astype(jnp.float32) * freq
        coarse_cos, coarse_sin = jnp.cos(coarse), jnp.sin(coarse)
        lanes = lax.broadcasted_iota(jnp.int32, (unit, 128), 1)
        sign = jnp.where(lanes < 64, -1.0, 1.0).astype(jnp.float32)
        for i in range(slots):
            c, s = coarse_cos[i : i + 1], coarse_sin[i : i + 1]
            cosine[group, pl.ds(i * unit, unit), :] = fine_cos * c - fine_sin * s
            sine[group, pl.ds(i * unit, unit), :] = (fine_sin * c + fine_cos * s) * sign
        for i in range(slots):
            rows = lax.broadcasted_iota(jnp.int32, (unit, tokens), 0) + i * unit
            cols = lax.broadcasted_iota(jnp.int32, (unit, tokens), 1)
            first = begins_of(jnp.full((1, tokens), i * unit, jnp.int32))
            allowed = (first <= cols) & (cols <= rows)
            bias[group, pl.ds(i * unit, unit), :] = jnp.where(allowed, 0.0, MASKED).astype(jnp.float32)

    def normalize(group, owner):
        step_rows = 64

        def step(i, carry):
            source = pl.ds(pl.multiple_of(i * step_rows, step_rows), step_rows)
            target = pl.ds(pl.multiple_of(owner * half_tokens + i * step_rows, step_rows), step_rows)
            q_part = lat[group, owner, source, 0:q_width].astype(jnp.float32)
            squares = jnp.mean(q_part * q_part, axis=-1, keepdims=True)
            qn[group, target, :] = (q_part * lax.rsqrt(squares + EPSILON) * q_gain[...]).astype(jnp.bfloat16)
            kv_part = lat[group, owner, source, q_width : q_width + kv_width].astype(jnp.float32)
            squares = jnp.mean(kv_part * kv_part, axis=-1, keepdims=True)
            kvn[group, target, :] = (kv_part * lax.rsqrt(squares + EPSILON) * kv_gain[...]).astype(jnp.bfloat16)
            tail = lat[group, owner, source, q_width + kv_width :].astype(jnp.float32)
            turned = tail * cosine[group, target, :] + pltpu.roll(tail, 64, 1) * sine[group, target, :]
            lanes = lax.broadcasted_iota(jnp.int32, turned.shape, 1)
            first = lax.rem(lanes, 64) < 32
            kr[group, 0, target, :] = jnp.where(first, turned, 0.0).astype(jnp.bfloat16)
            kr[group, 1, target, :] = jnp.where(first, 0.0, turned).astype(jnp.bfloat16)
            return carry

        lax.fori_loop(0, half_tokens // step_rows, step, 0)

    factor = (nope + rope) ** (-0.5) * math.log2(math.e)
    tile = tokens // 2

    def attend(block, group):
        for j in range(nh // 2):
            for r in range(2):
                rows = pl.ds(r * tile, tile)
                q = jnp.dot(
                    qn[group, rows, :], wq_buf[block, :, j * 384 : (j + 1) * 384],
                    preferred_element_type=jnp.float32,
                )
                tail = q[:, 2 * nope :]
                turned = tail * cosine[group, rows, :] + pltpu.roll(tail, 64, 1) * sine[group, rows, :]
                turned = turned.astype(jnp.bfloat16)
                for a in range(2):
                    q_s[a, rows, 0:nope] = q[:, a * nope : (a + 1) * nope].astype(jnp.bfloat16)
                    q_s[a, rows, nope:] = turned
                width = nope + vd
                kv = jnp.dot(
                    kvn[group, rows, :], wkv_buf[block, :, j * 2 * width : (j + 1) * 2 * width],
                    preferred_element_type=jnp.float32,
                ).astype(jnp.bfloat16)
                for a in range(2):
                    k_s[a, rows, 0:nope] = kv[:, a * width : a * width + nope]
                    k_s[a, rows, nope:] = kr[group, a, rows, :]
                    v_s[a, rows, :] = kv[:, a * width + nope : (a + 1) * width]
            for a in range(2):
                for r in range(2):
                    rows = pl.ds(r * tile, tile)
                    span = (r + 1) * tile
                    scores = lax.dot_general(
                        q_s[a, rows, :], k_s[a, 0:span, :], (((1,), (1,)), ((), ())),
                        preferred_element_type=jnp.float32,
                    )
                    scores = scores + bias[group, rows, 0:span]
                    top = jnp.max(scores, axis=-1, keepdims=True)
                    terms = jnp.exp2((scores - top) * factor)
                    total = jnp.sum(terms, axis=-1, keepdims=True)
                    mixed = jnp.dot(
                        terms.astype(jnp.bfloat16), v_s[a, 0:span, :], preferred_element_type=jnp.float32
                    )
                    at = (2 * j + a) * vd
                    obuf[group, block, rows, at : at + vd] = (mixed / total).astype(jnp.bfloat16)

    def columns(block):
        width = nh * vd
        return pl.ds(pl.multiple_of((2 * block + parity) * width, width), width)

    def local_out(block):
        return pltpu.make_async_copy(obuf.at[0, block], out.at[:, columns(block)], out_local.at[block])

    def pair_out(block):
        return pltpu.make_async_remote_copy(
            src_ref=obuf.at[1, block], dst_ref=out.at[:, columns(block)],
            send_sem=out_send.at[block], recv_sem=out_recv.at[block],
            device_id=pair, device_id_type=MESH,
        )

    def pair_out_wait(block):
        width = nh * vd
        span = pl.ds(pl.multiple_of((2 * block + 1 - parity) * width, width), width)
        return pltpu.make_async_remote_copy(
            src_ref=obuf.at[1, block], dst_ref=out.at[:, span],
            send_sem=out_send.at[block], recv_sem=out_recv.at[block],
            device_id=pair, device_id_type=MESH,
        )

    lax.fori_loop(0, 2, lambda g, c: (tables(g), c)[1], 0)
    own_lat.wait()
    normalize(0, core)
    lat_copy(latents, 0, 1 - core, sibling, 0).wait_recv()
    normalize(0, 1 - core)
    own_wq.wait()
    own_wkv.wait()

    def own_step(g, carry):
        @pl.when(g == 1)
        def _():
            forward(1, 0)
            lat_copy(latents, 1, core, pair, 1).wait_recv()
            lat_copy(lat.at[1, core], 1, core, sibling, 2).start()
            normalize(1, core)
            lat_copy(lat.at[1, 1 - core], 1, 1 - core, sibling, 2).wait_recv()
            normalize(1, 1 - core)
            forward(1, 1)

        attend(pos, g)
        return carry

    lax.fori_loop(0, 2, own_step, 0)
    local_out(pos).start()
    pair_out(pos).start()
    forward(1, 2)

    def stage(t, carry):
        @pl.when(t < n_line)
        def _():
            for chunk in range(CHUNKS):
                forward(t, chunk)

        def side(s, inner):
            block = pos + (2 * s - 1) * (t - 1)

            @pl.when((block >= 0) & (block < n_line))
            def _():
                held = jnp.clip(block, 0, n_line - 1)
                for chunk in range(CHUNKS):
                    x_copy(held, chunk, 1 - half).wait_recv()

                def group_step(i, rest):
                    attend(held, 1 - i)

                    @pl.when(i == 0)
                    def _():
                        pair_out(held).start()

                    return rest

                lax.fori_loop(0, 2, group_step, 0)
                local_out(held).start()

            return inner

        return lax.fori_loop(0, 2, side, carry)

    lax.fori_loop(2, n_line + 1, stage, 0)

    lat_copy(latents, 0, core, sibling, 0).wait_send()
    lat_copy(latents, 1, core, pair, 1).wait_send()
    lat_copy(lat.at[1, core], 1, core, sibling, 2).wait_send()

    def drain(block, carry):
        @pl.when((block <= pos) & has_right)
        def _():
            for chunk in range(CHUNKS):
                line_copy(block, chunk, 1).wait_send()

        @pl.when((block >= pos) & has_left)
        def _():
            for chunk in range(CHUNKS):
                line_copy(block, chunk, 0).wait_send()

        @pl.when(block != pos)
        def _():
            for chunk in range(CHUNKS):
                x_copy(block, chunk, half).wait_send()

        local_out(block).wait()
        pair_out(block).wait_send()
        pair_out_wait(block).wait_recv()
        return carry

    lax.fori_loop(0, n_line, drain, 0)


def shards(latents, q_gain, kv_gain, q_weight, kv_weight, lengths):
    q_width, kv_width = q_gain.shape[0], kv_gain.shape[0]
    rope = latents.shape[1] - q_width - kv_width
    nh = q_weight.shape[2]
    nope = q_weight.shape[3] - rope
    vd = kv_weight.shape[3] - nope
    n_seq = lax.axis_size("seq")
    n_line = n_seq // 2
    half_tokens = latents.shape[0]
    tokens = half_tokens * lax.axis_size("head")
    slots = lengths.shape[1]
    r = rope // 2

    body = q_width + kv_width
    first, second = latents[:, body : body + r], latents[:, body + r :]
    lat = jnp.concatenate([latents[:, :body], first, first, second, second], axis=1)
    wide = lat.shape[1]
    q4 = q_weight[0].reshape(q_width, nh // 2, 2, nope + rope)
    wq = jnp.concatenate(
        [
            q4[:, :, 0, :nope], q4[:, :, 1, :nope],
            q4[:, :, 0, nope : nope + r], q4[:, :, 1, nope : nope + r],
            q4[:, :, 0, nope + r :], q4[:, :, 1, nope + r :],
        ],
        axis=-1,
    ).reshape(q_width, nh * (nope + rope))
    wkv = kv_weight[0].reshape(kv_width, nh * (nope + vd))
    base = 10000.0 ** (-2.0 * np.arange(r) / rope)
    freqs = jnp.asarray(np.tile(base, 4)[None, :], jnp.float32)

    vmem = pl.BlockSpec(memory_space=pltpu.VMEM)
    hbm = pl.BlockSpec(memory_space=pl.ANY)
    bf16, f32, dma = jnp.bfloat16, jnp.float32, pltpu.SemaphoreType.DMA
    heads_total = nh * n_seq
    return pl.pallas_call(
        functools.partial(kernel, n_line, nh, q_width, kv_width, rope, nope, vd, tokens, slots),
        out_shape=jax.ShapeDtypeStruct((tokens, heads_total * vd), bf16),
        in_specs=[pl.BlockSpec(memory_space=pltpu.SMEM), vmem, vmem, vmem, hbm, hbm, hbm],
        out_specs=hbm,
        scratch_shapes=[
            pltpu.VMEM((n_line,) + wq.shape, bf16),
            pltpu.VMEM((n_line,) + wkv.shape, bf16),
            pltpu.VMEM((2, 2, half_tokens, wide), bf16),
            pltpu.VMEM((2, tokens, q_width), bf16),
            pltpu.VMEM((2, tokens, kv_width), bf16),
            pltpu.VMEM((2, tokens, 128), f32),
            pltpu.VMEM((2, tokens, 128), f32),
            pltpu.VMEM((2, 2, tokens, 128), bf16),
            pltpu.VMEM((2, tokens, tokens), f32),
            pltpu.VMEM((2, tokens, nope + 128), bf16),
            pltpu.VMEM((2, tokens, nope + 128), bf16),
            pltpu.VMEM((2, tokens, vd), bf16),
            pltpu.VMEM((2, n_line, tokens, nh * vd), bf16),
            dma((3,)), dma((3,)), dma((3,)),
            dma((2, n_line, CHUNKS)), dma((n_line, CHUNKS)),
            dma((n_line, CHUNKS)), dma((n_line, CHUNKS)),
            dma((n_line,)), dma((n_line,)), dma((n_line,)),
        ],
        compiler_params=pltpu.CompilerParams(
            collective_id=0, has_side_effects=True, vmem_limit_bytes=60 * 1024 * 1024
        ),
    )(lengths, freqs, q_gain[None, :], kv_gain[None, :], lat, wq, wkv)


def solution(mesh):
    return jax.shard_map(
        shards,
        mesh=mesh,
        in_specs=(
            P(("parts", "seq", "head"), None),
            P(),
            P(),
            P("head", None, "seq", None),
            P("head", None, "seq", None),
            P("parts", None),
        ),
        out_specs=P(("parts", "seq"), "head"),
        check_vma=False,
    )
```

```python
import functools
import math

import jax
import jax.numpy as jnp
import numpy as np
from jax import lax
from jax.experimental import pallas as pl
from jax.experimental.pallas import tpu as pltpu
from jax.sharding import PartitionSpec as P

EPSILON = 1e-06
MASKED = -1e30
CHUNKS = 6
MESH = pl.DeviceIdType.MESH


def kernel(
    n_line, nh, q_width, kv_width, rope, nope, vd, tokens, slots,
    lengths, freqs, q_gain, kv_gain, latents, wq, wkv,
    out,
    wq_buf, wkv_buf, lat, qn, kvn, cosine, sine, kr, bias, q_s, k_s, v_s, obuf,
    own_sem, lat_send, lat_recv, line_send, line_recv, x_send, x_recv, out_local, out_send, out_recv,
):
    part = lax.axis_index("parts")
    seq = lax.axis_index("seq")
    core = lax.axis_index("head")
    half = lax.rem(part, 2)
    pos = seq // 2
    parity = lax.rem(seq, 2)
    pair = {"seq": seq + 1 - 2 * parity}
    sibling = {"head": 1 - core}
    across = {"parts": part + 1 - 2 * half}
    left = {"seq": jnp.maximum(seq - 2, parity)}
    right = {"seq": jnp.minimum(seq + 2, 2 * (n_line - 1) + parity)}
    has_left = pos > 0
    has_right = pos < n_line - 1
    half_tokens = tokens // 2
    per = nh // 2
    split = per % 2 == 0
    head = nope + rope
    width = nope + vd
    r = rope // 2
    q_rows = nh * head // 8
    kv_rows = kv_width // 2

    def slot(block, side, chunk):
        if chunk < 4:
            start = pl.multiple_of(side * (4 * q_rows) + chunk * q_rows, q_rows)
            return wq_buf.at[block, pl.ds(start, q_rows), :]
        return wkv_buf.at[block, side, pl.ds((chunk - 4) * kv_rows, kv_rows), :]

    def line_copy(block, chunk, direction):
        return pltpu.make_async_remote_copy(
            src_ref=slot(block, half, chunk), dst_ref=slot(block, half, chunk),
            send_sem=line_send.at[direction, block, chunk], recv_sem=line_recv.at[block, chunk],
            device_id=(left, right)[direction], device_id_type=MESH,
        )

    def x_copy(block, chunk, side):
        return pltpu.make_async_remote_copy(
            src_ref=slot(block, side, chunk), dst_ref=slot(block, side, chunk),
            send_sem=x_send.at[block, chunk], recv_sem=x_recv.at[block, chunk],
            device_id=across, device_id_type=MESH,
        )

    def lat_copy(source, group, owner, target, index):
        return pltpu.make_async_remote_copy(
            src_ref=source, dst_ref=lat.at[group, owner],
            send_sem=lat_send.at[index], recv_sem=lat_recv.at[index],
            device_id=target, device_id_type=MESH,
        )

    barrier = pltpu.get_barrier_semaphore()
    for target in (pair, sibling, across):
        pl.semaphore_signal(barrier, inc=1, device_id=target, device_id_type=MESH)

    @pl.when(has_left)
    def _():
        pl.semaphore_signal(barrier, inc=1, device_id=left, device_id_type=MESH)

    @pl.when(has_right)
    def _():
        pl.semaphore_signal(barrier, inc=1, device_id=right, device_id_type=MESH)

    own_lat = pltpu.make_async_copy(latents, lat.at[0, core], own_sem.at[0])
    own = []
    for h in range(nh):
        j, a = h // 2, h % 2
        for start, size, at in (
            (0, nope, a * nope), (nope, r, 2 * nope + a * r), (nope + r, r, 2 * nope + 2 * r + a * r)
        ):
            own.append((wq.at[pl.ds(h * head + start, size), :], wq_buf.at[pos, pl.ds(2 * j * head + at, size), :]))
    for side in range(2):
        own.append((wkv.at[:, pl.ds(side * per * width, per * width)], wkv_buf.at[pos, side]))
    own = [pltpu.make_async_copy(*ends, own_sem.at[1 + i]) for i, ends in enumerate(own)]
    own_lat.start()
    for copy in own:
        copy.start()

    pl.semaphore_wait(barrier, 3 + has_left.astype(jnp.int32) + has_right.astype(jnp.int32))

    lat_copy(latents, 0, core, sibling, 0).start()
    lat_copy(latents, 1, core, pair, 1).start()
    for copy in own:
        copy.wait()

    @pl.when(has_left)
    def _():
        for chunk in range(CHUNKS):
            line_copy(pos, chunk, 0).start()

    @pl.when(has_right)
    def _():
        for chunk in range(CHUNKS):
            line_copy(pos, chunk, 1).start()

    def forward(distance, chunk):
        @pl.when(pos - distance >= 0)
        def _():
            block = jnp.maximum(pos - distance, 0)
            line_copy(block, chunk, 1).wait_recv()

            @pl.when(has_right)
            def _():
                line_copy(block, chunk, 1).start()

            x_copy(block, chunk, half).start()

        @pl.when(pos + distance < n_line)
        def _():
            block = jnp.minimum(pos + distance, n_line - 1)
            line_copy(block, chunk, 0).wait_recv()

            @pl.when(has_left)
            def _():
                line_copy(block, chunk, 0).start()

            x_copy(block, chunk, half).start()

    unit = tokens // slots

    def tables(group):
        index = jnp.where(group == 0, seq, seq + 1 - 2 * parity)
        spans = []
        begin = jnp.int32(0)
        for i in range(slots):
            end = begin + lengths[index, i]
            spans.append((begin, end))
            begin = end

        def begins_of(ids):
            found = jnp.zeros_like(ids)
            for low, high in spans:
                found = jnp.where((ids >= low) & (ids < high), low, found)
            return found

        freq = freqs[...]
        fine = lax.broadcasted_iota(jnp.int32, (unit, 128), 0).astype(jnp.float32) * freq
        fine_cos, fine_sin = jnp.cos(fine), jnp.sin(fine)
        coarse_ids = lax.broadcasted_iota(jnp.int32, (slots, 128), 0) * unit
        coarse = (coarse_ids - begins_of(coarse_ids)).astype(jnp.float32) * freq
        coarse_cos, coarse_sin = jnp.cos(coarse), jnp.sin(coarse)
        lanes = lax.broadcasted_iota(jnp.int32, (unit, 128), 1)
        sign = jnp.where(lanes < 64, -1.0, 1.0).astype(jnp.float32)
        for i in range(slots):
            c, s = coarse_cos[i : i + 1], coarse_sin[i : i + 1]
            cosine[group, pl.ds(i * unit, unit), :] = fine_cos * c - fine_sin * s
            sine[group, pl.ds(i * unit, unit), :] = (fine_sin * c + fine_cos * s) * sign
        for i in range(slots):
            rows = lax.broadcasted_iota(jnp.int32, (unit, tokens), 0) + i * unit
            cols = lax.broadcasted_iota(jnp.int32, (unit, tokens), 1)
            first = begins_of(jnp.full((1, tokens), i * unit, jnp.int32))
            allowed = (first <= cols) & (cols <= rows)
            bias[group, pl.ds(i * unit, unit), :] = jnp.where(allowed, 0.0, MASKED).astype(jnp.float32)

    def normalize(group, owner):
        step_rows = 64

        def step(i, carry):
            source = pl.ds(pl.multiple_of(i * step_rows, step_rows), step_rows)
            target = pl.ds(pl.multiple_of(owner * half_tokens + i * step_rows, step_rows), step_rows)
            q_part = lat[group, owner, source, 0:q_width].astype(jnp.float32)
            squares = jnp.mean(q_part * q_part, axis=-1, keepdims=True)
            qn[group, target, :] = (q_part * lax.rsqrt(squares + EPSILON) * q_gain[...]).astype(jnp.bfloat16)
            kv_part = lat[group, owner, source, q_width : q_width + kv_width].astype(jnp.float32)
            squares = jnp.mean(kv_part * kv_part, axis=-1, keepdims=True)
            kvn[group, target, :] = (kv_part * lax.rsqrt(squares + EPSILON) * kv_gain[...]).astype(jnp.bfloat16)
            tail = lat[group, owner, source, q_width + kv_width :].astype(jnp.float32)
            tail = jnp.concatenate([tail, tail], axis=1)
            lanes = lax.broadcasted_iota(jnp.int32, tail.shape, 1)
            tail = jnp.where((lanes >= r) & (lanes < 3 * r), pltpu.roll(tail, r, 1), tail)
            turned = tail * cosine[group, target, :] + pltpu.roll(tail, 64, 1) * sine[group, target, :]
            first = lax.rem(lanes, 64) < 32
            kr[group, 0, target, :] = jnp.where(first, turned, 0.0).astype(jnp.bfloat16)
            kr[group, 1, target, :] = jnp.where(first, 0.0, turned).astype(jnp.bfloat16)
            return carry

        lax.fori_loop(0, half_tokens // step_rows, step, 0)

    factor = (nope + rope) ** (-0.5) * math.log2(math.e)
    tile = tokens // 2

    def attend(block, group, j):
        q_at = pl.ds(pl.multiple_of(j * 2 * head, 2 * head), 2 * head)
        for i in range(2):
            rows = pl.ds(i * tile, tile)
            q = lax.dot_general(
                qn[group, rows, :], wq_buf[block, q_at, :], (((1,), (1,)), ((), ())),
                preferred_element_type=jnp.float32,
            )
            tail = q[:, 2 * nope :]
            turned = tail * cosine[group, rows, :] + pltpu.roll(tail, 64, 1) * sine[group, rows, :]
            turned = turned.astype(jnp.bfloat16)
            for a in range(2):
                q_s[a, rows, 0:nope] = q[:, a * nope : (a + 1) * nope].astype(jnp.bfloat16)
                q_s[a, rows, nope:] = turned
                if split:
                    side, at = j // (per // 2), lax.rem(j, per // 2) * 2 + a
                else:
                    side, at = (2 * j + a) // per, lax.rem(2 * j + a, per)
                if per <= 2:
                    at = a if split else 0
                    kv_at = pl.ds(at * width, width)
                else:
                    kv_at = pl.ds(pl.multiple_of(at * width, width), width)
                kv = jnp.dot(
                    kvn[group, rows, :], wkv_buf[block, side, :, kv_at],
                    preferred_element_type=jnp.float32,
                ).astype(jnp.bfloat16)
                k_s[a, rows, 0:nope] = kv[:, 0:nope]
                k_s[a, rows, nope:] = kr[group, a, rows, :]
                v_s[a, rows, :] = kv[:, nope:]
        for a in range(2):
            for i in range(2):
                rows = pl.ds(i * tile, tile)
                span = (i + 1) * tile
                scores = lax.dot_general(
                    q_s[a, rows, :], k_s[a, 0:span, :], (((1,), (1,)), ((), ())),
                    preferred_element_type=jnp.float32,
                )
                scores = scores + bias[group, rows, 0:span]
                top = jnp.max(scores, axis=-1, keepdims=True)
                terms = jnp.exp2((scores - top) * factor)
                total = jnp.sum(terms, axis=-1, keepdims=True)
                mixed = jnp.dot(
                    terms.astype(jnp.bfloat16), v_s[a, 0:span, :], preferred_element_type=jnp.float32
                )
                obuf[group, block, j, rows, a * vd : (a + 1) * vd] = (mixed / total).astype(jnp.bfloat16)

    def columns(owner, block, j):
        return pl.ds(pl.multiple_of(((2 * block + owner) * per + j) * 2 * vd, 2 * vd), 2 * vd)

    def local_out(block, j):
        return pltpu.make_async_copy(
            obuf.at[0, block, j], out.at[:, columns(parity, block, j)], out_local.at[block, j]
        )

    def pair_out(block, j, owner):
        return pltpu.make_async_remote_copy(
            src_ref=obuf.at[1, block, j], dst_ref=out.at[:, columns(owner, block, j)],
            send_sem=out_send.at[block, j], recv_sem=out_recv.at[block, j],
            device_id=pair, device_id_type=MESH,
        )

    lax.fori_loop(0, 2, lambda g, c: (tables(g), c)[1], 0)
    own_lat.wait()
    normalize(0, core)
    lat_copy(latents, 0, 1 - core, sibling, 0).wait_recv()
    normalize(0, 1 - core)
    forward(1, 0)

    def own_step(u, carry):
        g, j = u // per, lax.rem(u, per)

        @pl.when(u == per)
        def _():
            forward(1, 2)
            lat_copy(latents, 1, core, pair, 1).wait_recv()
            lat_copy(lat.at[1, core], 1, core, sibling, 2).start()
            forward(1, 3)
            normalize(1, core)
            lat_copy(lat.at[1, 1 - core], 1, 1 - core, sibling, 2).wait_recv()
            normalize(1, 1 - core)
            forward(1, 4)

        attend(pos, g, j)

        @pl.when(u == 0)
        def _():
            forward(1, 1)

        @pl.when(g == 0)
        def _():
            local_out(pos, j).start()

        @pl.when(g == 1)
        def _():
            pair_out(pos, j, parity).start()

        return carry

    lax.fori_loop(0, 2 * per, own_step, 0)
    forward(1, 5)

    def work(t, first, count, wait):
        def side(n, inner):
            block = pos + (2 * n - 1) * t

            @pl.when((block >= 0) & (block < n_line))
            def _():
                held = jnp.clip(block, 0, n_line - 1)

                @pl.when(wait)
                def _():
                    for chunk in range(CHUNKS):
                        x_copy(held, chunk, 1 - half).wait_recv()

                def unit_step(i, rest):
                    j, g = first + i // 2, 1 - lax.rem(i, 2)
                    attend(held, g, j)

                    @pl.when(g == 1)
                    def _():
                        pair_out(held, j, parity).start()

                    @pl.when(g == 0)
                    def _():
                        local_out(held, j).start()

                    return rest

                lax.fori_loop(0, 2 * count, unit_step, 0)

            return inner

        lax.fori_loop(0, 2, side, 0)

    def stage(i, carry):
        t, late = i // 2, lax.rem(i, 2) == 0

        @pl.when(late & (t < n_line))
        def _():
            for chunk in range(CHUNKS):
                forward(t, chunk)

        if split:
            count = per // 2
            first = jnp.where(late, 1 - half, half) * count
            work(jnp.where(late, t - 1, t), first, count, late)
        else:

            @pl.when(late)
            def _():
                work(t - 1, 0, per, late)

        return carry

    lax.fori_loop(4 - int(split), 2 * n_line + 1, stage, 0)

    lat_copy(latents, 0, core, sibling, 0).wait_send()
    lat_copy(latents, 1, core, pair, 1).wait_send()
    lat_copy(lat.at[1, core], 1, core, sibling, 2).wait_send()

    def drain(block, carry):
        @pl.when((block <= pos) & has_right)
        def _():
            for chunk in range(CHUNKS):
                line_copy(block, chunk, 1).wait_send()

        @pl.when((block >= pos) & has_left)
        def _():
            for chunk in range(CHUNKS):
                line_copy(block, chunk, 0).wait_send()

        @pl.when(block != pos)
        def _():
            for chunk in range(CHUNKS):
                x_copy(block, chunk, half).wait_send()

        for j in range(per):
            local_out(block, j).wait()
            pair_out(block, j, parity).wait_send()
            pair_out(block, j, 1 - parity).wait_recv()
        return carry

    lax.fori_loop(0, n_line, drain, 0)


def shards(latents, q_gain, kv_gain, q_weight, kv_weight, lengths):
    q_width, kv_width = q_gain.shape[0], kv_gain.shape[0]
    rope = latents.shape[1] - q_width - kv_width
    nh = q_weight.shape[2]
    nope = q_weight.shape[3] - rope
    vd = kv_weight.shape[3] - nope
    n_seq = lax.axis_size("seq")
    n_line = n_seq // 2
    half_tokens = latents.shape[0]
    tokens = half_tokens * lax.axis_size("head")
    slots = lengths.shape[1]
    r = rope // 2

    wide = latents.shape[1]
    wq = jnp.transpose(q_weight[0], (1, 2, 0)).reshape(nh * (nope + rope), q_width)
    wkv = kv_weight[0].reshape(kv_width, nh * (nope + vd))
    base = 10000.0 ** (-2.0 * np.arange(r) / rope)
    freqs = jnp.asarray(np.tile(base, 4)[None, :], jnp.float32)

    vmem = pl.BlockSpec(memory_space=pltpu.VMEM)
    hbm = pl.BlockSpec(memory_space=pl.ANY)
    bf16, f32, dma = jnp.bfloat16, jnp.float32, pltpu.SemaphoreType.DMA
    heads_total = nh * n_seq
    return pl.pallas_call(
        functools.partial(kernel, n_line, nh, q_width, kv_width, rope, nope, vd, tokens, slots),
        out_shape=jax.ShapeDtypeStruct((tokens, heads_total * vd), bf16),
        in_specs=[pl.BlockSpec(memory_space=pltpu.SMEM), vmem, vmem, vmem, hbm, hbm, hbm],
        out_specs=hbm,
        scratch_shapes=[
            pltpu.VMEM((n_line,) + wq.shape, bf16),
            pltpu.VMEM((n_line, 2, kv_width, nh * (nope + vd) // 2), bf16),
            pltpu.VMEM((2, 2, half_tokens, wide), bf16),
            pltpu.VMEM((2, tokens, q_width), bf16),
            pltpu.VMEM((2, tokens, kv_width), bf16),
            pltpu.VMEM((2, tokens, 128), f32),
            pltpu.VMEM((2, tokens, 128), f32),
            pltpu.VMEM((2, 2, tokens, 128), bf16),
            pltpu.VMEM((2, tokens, tokens), f32),
            pltpu.VMEM((2, tokens, nope + 128), bf16),
            pltpu.VMEM((2, tokens, nope + 128), bf16),
            pltpu.VMEM((2, tokens, vd), bf16),
            pltpu.VMEM((2, n_line, nh // 2, tokens, 2 * vd), bf16),
            dma((3 * nh + 3,)), dma((3,)), dma((3,)),
            dma((2, n_line, CHUNKS)), dma((n_line, CHUNKS)),
            dma((n_line, CHUNKS)), dma((n_line, CHUNKS)),
            dma((n_line, nh // 2)), dma((n_line, nh // 2)), dma((n_line, nh // 2)),
        ],
        compiler_params=pltpu.CompilerParams(
            collective_id=0, has_side_effects=True, vmem_limit_bytes=60 * 1024 * 1024
        ),
    )(lengths, freqs, q_gain[None, :], kv_gain[None, :], latents, wq, wkv)


def solution(mesh):
    return jax.shard_map(
        shards,
        mesh=mesh,
        in_specs=(
            P(("parts", "seq", "head"), None),
            P(),
            P(),
            P("head", None, "seq", None),
            P("head", None, "seq", None),
            P("parts", None),
        ),
        out_specs=P(("parts", "seq"), "head"),
        check_vma=False,
    )
```

```python
import functools
import math

import jax
import jax.numpy as jnp
import numpy as np
from jax import lax
from jax.experimental import pallas as pl
from jax.experimental.pallas import tpu as pltpu
from jax.sharding import PartitionSpec as P

EPSILON = 1e-06
MASKED = -1e30
CHUNKS = 6
MESH = pl.DeviceIdType.MESH


def kernel(
    n_line, nh, q_width, kv_width, rope, nope, vd, tokens, slots,
    lengths, freqs, q_gain, kv_gain, latents, wq, wkv,
    out,
    wq_buf, wkv_buf, lat, qn, kvn, cosine, sine, kr, bias, q_s, k_s, v_s, obuf, gains, turned_lat,
    own_sem, lat_send, lat_recv, line_send, line_recv, x_send, x_recv, out_send, out_recv,
):
    part = lax.axis_index("parts")
    seq = lax.axis_index("seq")
    core = lax.axis_index("head")
    half = lax.rem(part, 2)
    pos = seq // 2
    parity = lax.rem(seq, 2)
    pair = {"seq": seq + 1 - 2 * parity}
    sibling = {"head": 1 - core}
    across = {"parts": part + 1 - 2 * half}
    left = {"seq": jnp.maximum(seq - 2, parity)}
    right = {"seq": jnp.minimum(seq + 2, 2 * (n_line - 1) + parity)}
    has_left = pos > 0
    has_right = pos < n_line - 1
    half_tokens = tokens // 2
    per = nh // 2
    split = per % 2 == 0
    head = nope + rope
    width = nope + vd
    r = rope // 2
    q_rows = nh * head // 8
    kv_rows = kv_width // 2

    def slot(block, side, chunk):
        if chunk < 4:
            start = pl.multiple_of(side * (4 * q_rows) + chunk * q_rows, q_rows)
            return wq_buf.at[block, pl.ds(start, q_rows), :]
        return wkv_buf.at[block, side, pl.ds((chunk - 4) * kv_rows, kv_rows), :]

    def at_end(block):
        return (block == 0) | (block == n_line - 1)

    def line_copy(block, chunk, direction):
        held = slot(block, half, chunk) if chunk < CHUNKS else slot(block, 1 - half, CHUNKS - 1)
        return pltpu.make_async_remote_copy(
            src_ref=held, dst_ref=held,
            send_sem=line_send.at[direction, block, chunk], recv_sem=line_recv.at[block, chunk],
            device_id=(left, right)[direction], device_id_type=MESH,
        )

    def x_copy(block, chunk, side):
        return pltpu.make_async_remote_copy(
            src_ref=slot(block, side, chunk), dst_ref=slot(block, side, chunk),
            send_sem=x_send.at[block, chunk], recv_sem=x_recv.at[block, chunk],
            device_id=across, device_id_type=MESH,
        )

    def lat_copy(source, group, owner, target, index):
        return pltpu.make_async_remote_copy(
            src_ref=source, dst_ref=lat.at[group, owner],
            send_sem=lat_send.at[index], recv_sem=lat_recv.at[index],
            device_id=target, device_id_type=MESH,
        )

    barrier = pltpu.get_barrier_semaphore()
    for target in (pair, sibling, across):
        pl.semaphore_signal(barrier, inc=1, device_id=target, device_id_type=MESH)

    @pl.when(has_left)
    def _():
        pl.semaphore_signal(barrier, inc=1, device_id=left, device_id_type=MESH)

    @pl.when(has_right)
    def _():
        pl.semaphore_signal(barrier, inc=1, device_id=right, device_id_type=MESH)

    own_lat = pltpu.make_async_copy(latents, turned_lat, own_sem.at[0])
    own = []
    for h in range(nh):
        j, a = h // 2, h % 2
        for start, size, at in (
            (0, nope, a * nope), (nope, r, 2 * nope + a * r), (nope + r, r, 2 * nope + 2 * r + a * r)
        ):
            own.append((wq.at[pl.ds(h * head + start, size), :], wq_buf.at[pos, pl.ds(2 * j * head + at, size), :]))
    for side in range(2):
        own.append((wkv.at[:, pl.ds(side * per * width, per * width)], wkv_buf.at[pos, side]))
    own = [pltpu.make_async_copy(*ends, own_sem.at[1 + i]) for i, ends in enumerate(own)]
    own_lat.start()
    for copy in own:
        copy.start()

    pl.semaphore_wait(barrier, 3 + has_left.astype(jnp.int32) + has_right.astype(jnp.int32))

    for copy in own:
        copy.wait()

    @pl.when(has_left)
    def _():
        for chunk in range(CHUNKS):
            line_copy(pos, chunk, 0).start()

        @pl.when(at_end(pos))
        def _():
            line_copy(pos, CHUNKS, 0).start()

    @pl.when(has_right)
    def _():
        for chunk in range(CHUNKS):
            line_copy(pos, chunk, 1).start()

        @pl.when(at_end(pos))
        def _():
            line_copy(pos, CHUNKS, 1).start()

    def pass_on(block, chunk, direction):
        line_copy(block, chunk, 1 - direction).wait_recv()

        @pl.when((has_left, has_right)[direction])
        def _():
            line_copy(block, chunk, direction).start()

        if chunk < CHUNKS - 1:
            x_copy(block, chunk, half).start()
        elif chunk == CHUNKS - 1:

            @pl.when(jnp.logical_not(at_end(block)))
            def _():
                x_copy(block, chunk, half).start()

    def forward(distance, chunk):
        def both(condition, block, direction):
            if chunk == CHUNKS:
                condition = condition & at_end(block)

            @pl.when(condition)
            def _():
                pass_on(block, chunk, direction)

        both(pos - distance >= 0, jnp.maximum(pos - distance, 0), 1)
        both(pos + distance < n_line, jnp.minimum(pos + distance, n_line - 1), 0)

    unit = tokens // slots

    def tables(group):
        index = jnp.where(group == 0, seq, seq + 1 - 2 * parity)
        spans = []
        begin = jnp.int32(0)
        for i in range(slots):
            end = begin + lengths[index, i]
            spans.append((begin, end))
            begin = end

        def begins_of(ids):
            found = jnp.zeros_like(ids)
            for low, high in spans:
                found = jnp.where((ids >= low) & (ids < high), low, found)
            return found

        freq = freqs[...]
        fine = lax.broadcasted_iota(jnp.int32, (unit, 128), 0).astype(jnp.float32) * freq
        fine_cos, fine_sin = jnp.cos(fine), jnp.sin(fine)
        coarse_ids = lax.broadcasted_iota(jnp.int32, (slots, 128), 0) * unit
        coarse = (coarse_ids - begins_of(coarse_ids)).astype(jnp.float32) * freq
        coarse_cos, coarse_sin = jnp.cos(coarse), jnp.sin(coarse)
        lanes = lax.broadcasted_iota(jnp.int32, (unit, 128), 1)
        sign = jnp.where(lanes < 64, -1.0, 1.0).astype(jnp.float32)
        for i in range(slots):
            c, s = coarse_cos[i : i + 1], coarse_sin[i : i + 1]
            cosine[group, pl.ds(i * unit, unit), :] = fine_cos * c - fine_sin * s
            sine[group, pl.ds(i * unit, unit), :] = (fine_sin * c + fine_cos * s) * sign
        for i in range(slots):
            rows = lax.broadcasted_iota(jnp.int32, (unit, tokens), 0) + i * unit
            cols = lax.broadcasted_iota(jnp.int32, (unit, tokens), 1)
            first = begins_of(jnp.full((1, tokens), i * unit, jnp.int32))
            allowed = (first <= cols) & (cols <= rows)
            bias[group, pl.ds(i * unit, unit), :] = jnp.where(allowed, 0.0, MASKED).astype(jnp.float32)

    def normalize(group, owner):
        step_rows = 64

        def step(i, carry):
            source = pl.ds(pl.multiple_of(i * step_rows, step_rows), step_rows)
            target = pl.ds(pl.multiple_of(owner * half_tokens + i * step_rows, step_rows), step_rows)
            q_part = lat[group, owner, source, 0:q_width].astype(jnp.float32)
            squares = jnp.mean(q_part * q_part, axis=-1, keepdims=True)
            qn[group, target, :] = (q_part * lax.rsqrt(squares + EPSILON) * gains[0:1, 0:q_width]).astype(jnp.bfloat16)
            kv_part = lat[group, owner, source, q_width : q_width + kv_width].astype(jnp.float32)
            squares = jnp.mean(kv_part * kv_part, axis=-1, keepdims=True)
            kvn[group, target, :] = (kv_part * lax.rsqrt(squares + EPSILON) * gains[0:1, q_width : q_width + kv_width]).astype(jnp.bfloat16)
            tail = lat[group, owner, source, q_width + kv_width :].astype(jnp.float32)
            tail = jnp.concatenate([tail, tail], axis=1)
            lanes = lax.broadcasted_iota(jnp.int32, tail.shape, 1)
            tail = jnp.where((lanes >= r) & (lanes < 3 * r), pltpu.roll(tail, r, 1), tail)
            turned = tail * cosine[group, target, :] + pltpu.roll(tail, 64, 1) * sine[group, target, :]
            first = lax.rem(lanes, 64) < 32
            kr[group, 0, target, :] = jnp.where(first, turned, 0.0).astype(jnp.bfloat16)
            kr[group, 1, target, :] = jnp.where(first, 0.0, turned).astype(jnp.bfloat16)
            return carry

        lax.fori_loop(0, half_tokens // step_rows, step, 0)

    factor = (nope + rope) ** (-0.5) * math.log2(math.e)
    tile = tokens // 2

    def attend(block, group, j):
        q_at = pl.ds(pl.multiple_of(j * 2 * head, 2 * head), 2 * head)
        for i in range(2):
            rows = pl.ds(i * tile, tile)
            q = lax.dot_general(
                qn[group, rows, :], wq_buf[block, q_at, :], (((1,), (1,)), ((), ())),
                preferred_element_type=jnp.float32,
            )
            tail = q[:, 2 * nope :]
            turned = tail * cosine[group, rows, :] + pltpu.roll(tail, 64, 1) * sine[group, rows, :]
            turned = turned.astype(jnp.bfloat16)
            for a in range(2):
                q_s[a, rows, 0:nope] = q[:, a * nope : (a + 1) * nope].astype(jnp.bfloat16)
                q_s[a, rows, nope:] = turned
                if split:
                    side, at = j // (per // 2), lax.rem(j, per // 2) * 2 + a
                else:
                    side, at = (2 * j + a) // per, lax.rem(2 * j + a, per)
                if per <= 2:
                    at = a if split else 0
                    kv_at = pl.ds(at * width, width)
                else:
                    kv_at = pl.ds(pl.multiple_of(at * width, width), width)
                kv = jnp.dot(
                    kvn[group, rows, :], wkv_buf[block, side, :, kv_at],
                    preferred_element_type=jnp.float32,
                ).astype(jnp.bfloat16)
                k_s[a, rows, 0:nope] = kv[:, 0:nope]
                k_s[a, rows, nope:] = kr[group, a, rows, :]
                v_s[a, rows, :] = kv[:, nope:]
        for a in range(2):
            for i in range(2):
                rows = pl.ds(i * tile, tile)
                span = (i + 1) * tile
                scores = lax.dot_general(
                    q_s[a, rows, :], k_s[a, 0:span, :], (((1,), (1,)), ((), ())),
                    preferred_element_type=jnp.float32,
                )
                scores = scores + bias[group, rows, 0:span]
                top = jnp.max(scores, axis=-1, keepdims=True)
                terms = jnp.exp2((scores - top) * factor)
                total = jnp.sum(terms, axis=-1, keepdims=True)
                mixed = jnp.dot(
                    terms.astype(jnp.bfloat16), v_s[a, 0:span, :], preferred_element_type=jnp.float32
                )
                mixed = (mixed / total).astype(jnp.bfloat16)
                at = pl.multiple_of(((2 * block + parity) * per + j) * 2 * vd + a * vd, vd)

                @pl.when(group == 0)
                def _():
                    out[rows, pl.ds(at, vd)] = mixed

                @pl.when(group == 1)
                def _():
                    obuf[block, j, rows, a * vd : (a + 1) * vd] = mixed

    def columns(owner, block, j):
        return pl.ds(pl.multiple_of(((2 * block + owner) * per + j) * 2 * vd, 2 * vd), 2 * vd)

    def pair_out(block, j, owner):
        return pltpu.make_async_remote_copy(
            src_ref=obuf.at[block, j], dst_ref=out.at[:, columns(owner, block, j)],
            send_sem=out_send.at[block, j], recv_sem=out_recv.at[block, j],
            device_id=pair, device_id_type=MESH,
        )

    own_lat.wait()
    wide = turned_lat.shape[0]
    for low in range(0, wide, 128):
        high = min(low + 128, wide)
        lat[0, core, :, low:high] = turned_lat[low:high, :].T
    gains[0:1, 0:q_width] = q_gain[...].reshape(1, q_width)
    gains[0:1, q_width:] = kv_gain[...].reshape(1, kv_width)
    lax.fori_loop(0, 2, lambda g, c: (tables(g), c)[1], 0)
    lat_copy(lat.at[0, core], 0, core, sibling, 0).start()
    lat_copy(lat.at[0, core], 1, core, pair, 1).start()
    normalize(0, core)
    lat_copy(lat.at[0, core], 0, 1 - core, sibling, 0).wait_recv()
    normalize(0, 1 - core)
    forward(1, 0)

    def own_step(u, carry):
        g, j = u // per, lax.rem(u, per)

        @pl.when(u == per)
        def _():
            forward(1, 2)
            lat_copy(lat.at[0, core], 1, core, pair, 1).wait_recv()
            lat_copy(lat.at[1, core], 1, core, sibling, 2).start()
            forward(1, 3)
            normalize(1, core)
            lat_copy(lat.at[1, 1 - core], 1, 1 - core, sibling, 2).wait_recv()
            normalize(1, 1 - core)
            forward(1, 4)

        attend(pos, g, j)

        @pl.when(u == 0)
        def _():
            forward(1, 1)

        @pl.when(g == 1)
        def _():
            pair_out(pos, j, parity).start()

        return carry

    lax.fori_loop(0, 2 * per, own_step, 0)
    forward(1, 5)
    forward(1, CHUNKS)

    def work(t, first, count, wait):
        def side(n, inner):
            block = pos + (2 * n - 1) * t

            @pl.when((block >= 0) & (block < n_line))
            def _():
                held = jnp.clip(block, 0, n_line - 1)

                @pl.when(wait)
                def _():
                    for chunk in range(CHUNKS - 1):
                        x_copy(held, chunk, 1 - half).wait_recv()

                    @pl.when(jnp.logical_not(at_end(held)))
                    def _():
                        x_copy(held, CHUNKS - 1, 1 - half).wait_recv()

                def unit_step(i, rest):
                    j, g = first + i // 2, 1 - lax.rem(i, 2)
                    attend(held, g, j)

                    @pl.when(g == 1)
                    def _():
                        pair_out(held, j, parity).start()

                    return rest

                lax.fori_loop(0, 2 * count, unit_step, 0)

            return inner

        lax.fori_loop(0, 2, side, 0)

    def stage(i, carry):
        t, late = i // 2, lax.rem(i, 2) == 0

        @pl.when(late & (t < n_line))
        def _():
            for chunk in range(CHUNKS + 1):
                forward(t, chunk)

        if split:
            count = per // 2
            first = jnp.where(late, 1 - half, half) * count
            work(jnp.where(late, t - 1, t), first, count, late)
        else:

            @pl.when(late)
            def _():
                work(t - 1, 0, per, late)

        return carry

    lax.fori_loop(4 - int(split), 2 * n_line + 1, stage, 0)

    lat_copy(lat.at[0, core], 0, core, sibling, 0).wait_send()
    lat_copy(lat.at[0, core], 1, core, pair, 1).wait_send()
    lat_copy(lat.at[1, core], 1, core, sibling, 2).wait_send()

    def drain(block, carry):
        for goes, direction in (((block <= pos) & has_right, 1), ((block >= pos) & has_left, 0)):

            @pl.when(goes)
            def _():
                for chunk in range(CHUNKS):
                    line_copy(block, chunk, direction).wait_send()

                @pl.when(at_end(block))
                def _():
                    line_copy(block, CHUNKS, direction).wait_send()

        @pl.when(block != pos)
        def _():
            for chunk in range(CHUNKS - 1):
                x_copy(block, chunk, half).wait_send()

            @pl.when(jnp.logical_not(at_end(block)))
            def _():
                x_copy(block, CHUNKS - 1, half).wait_send()

        for j in range(per):
            pair_out(block, j, parity).wait_send()
            pair_out(block, j, 1 - parity).wait_recv()
        return carry

    lax.fori_loop(0, n_line, drain, 0)


def shards(latents, q_gain, kv_gain, q_weight, kv_weight, lengths):
    q_width, kv_width = q_gain.shape[0], kv_gain.shape[0]
    rope = latents.shape[1] - q_width - kv_width
    nh = q_weight.shape[2]
    nope = q_weight.shape[3] - rope
    vd = kv_weight.shape[3] - nope
    n_seq = lax.axis_size("seq")
    n_line = n_seq // 2
    half_tokens = latents.shape[0]
    tokens = half_tokens * lax.axis_size("head")
    slots = lengths.shape[1]
    r = rope // 2

    wide = latents.shape[1]
    wq = jnp.transpose(q_weight[0], (1, 2, 0)).reshape(nh * (nope + rope), q_width)
    wkv = kv_weight[0].reshape(kv_width, nh * (nope + vd))
    base = 10000.0 ** (-2.0 * np.arange(r) / rope)
    freqs = jnp.asarray(np.tile(base, 4)[None, :], jnp.float32)

    vmem = pl.BlockSpec(memory_space=pltpu.VMEM)
    hbm = pl.BlockSpec(memory_space=pl.ANY)
    bf16, f32, dma = jnp.bfloat16, jnp.float32, pltpu.SemaphoreType.DMA
    heads_total = nh * n_seq
    return pl.pallas_call(
        functools.partial(kernel, n_line, nh, q_width, kv_width, rope, nope, vd, tokens, slots),
        out_shape=pltpu.VMEM((tokens, heads_total * vd), bf16),
        in_specs=[pl.BlockSpec(memory_space=pltpu.SMEM), vmem, vmem, vmem, hbm, hbm, hbm],
        out_specs=vmem,
        scratch_shapes=[
            pltpu.VMEM((n_line,) + wq.shape, bf16),
            pltpu.VMEM((n_line, 2, kv_width, nh * (nope + vd) // 2), bf16),
            pltpu.VMEM((2, 2, half_tokens, wide), bf16),
            pltpu.VMEM((2, tokens, q_width), bf16),
            pltpu.VMEM((2, tokens, kv_width), bf16),
            pltpu.VMEM((2, tokens, 128), f32),
            pltpu.VMEM((2, tokens, 128), f32),
            pltpu.VMEM((2, 2, tokens, 128), bf16),
            pltpu.VMEM((2, tokens, tokens), f32),
            pltpu.VMEM((2, tokens, nope + 128), bf16),
            pltpu.VMEM((2, tokens, nope + 128), bf16),
            pltpu.VMEM((2, tokens, vd), bf16),
            pltpu.VMEM((n_line, nh // 2, tokens, 2 * vd), bf16),
            pltpu.VMEM((8, q_width + kv_width), f32),
            pltpu.VMEM((wide, half_tokens), bf16),
            dma((3 * nh + 3,)), dma((3,)), dma((3,)),
            dma((2, n_line, CHUNKS + 1)), dma((n_line, CHUNKS + 1)),
            dma((n_line, CHUNKS)), dma((n_line, CHUNKS)),
            dma((n_line, nh // 2)), dma((n_line, nh // 2)),
        ],
        compiler_params=pltpu.CompilerParams(
            collective_id=0, has_side_effects=True, vmem_limit_bytes=59 * 1024 * 1024
        ),
    )(lengths, freqs, q_gain, kv_gain, latents.T, wq, wkv)


def solution(mesh):
    return jax.shard_map(
        shards,
        mesh=mesh,
        in_specs=(
            P(("parts", "seq", "head"), None),
            P(),
            P(),
            P("head", None, "seq", None),
            P("head", None, "seq", None),
            P("parts", None),
        ),
        out_specs=P(("parts", "seq"), "head"),
        check_vma=False,
    )
```

```python
import functools
import math

import jax
import jax.numpy as jnp
import numpy as np
from jax import lax
from jax.experimental import pallas as pl
from jax.experimental.pallas import tpu as pltpu
from jax.sharding import PartitionSpec as P

EPSILON = 1e-06
MASKED = -1e30
CHUNKS = 6
EXTRA = 3
MESH = pl.DeviceIdType.MESH


def kernel(
    n_line, nh, q_width, kv_width, rope, nope, vd, tokens, slots,
    lengths, freqs, q_gain, kv_gain, latents, wq, wkv,
    out,
    wq_buf, wkv_buf, lat, qn, kvn, cosine, sine, kr, bias, q_s, k_s, v_s, obuf, gains, turned_lat,
    own_sem, lat_send, lat_recv, line_send, line_recv, x_send, x_recv, out_send, out_recv,
):
    part = lax.axis_index("parts")
    seq = lax.axis_index("seq")
    core = lax.axis_index("head")
    half = lax.rem(part, 2)
    pos = seq // 2
    parity = lax.rem(seq, 2)
    pair = {"seq": seq + 1 - 2 * parity}
    sibling = {"head": 1 - core}
    across = {"parts": part + 1 - 2 * half}
    left = {"seq": jnp.maximum(seq - 2, parity)}
    right = {"seq": jnp.minimum(seq + 2, 2 * (n_line - 1) + parity)}
    has_left = pos > 0
    has_right = pos < n_line - 1
    half_tokens = tokens // 2
    per = nh // 2
    split = per % 2 == 0
    head = nope + rope
    width = nope + vd
    r = rope // 2
    q_rows = nh * head // 8
    kv_rows = kv_width // 2

    def slot(block, side, chunk):
        if chunk < 4:
            start = pl.multiple_of(side * (4 * q_rows) + chunk * q_rows, q_rows)
            return wq_buf.at[block, pl.ds(start, q_rows), :]
        return wkv_buf.at[block, side, pl.ds((chunk - 4) * kv_rows, kv_rows), :]

    def at_end(block):
        return (block == 0) | (block == n_line - 1)

    def direct(block):
        return at_end(block) & (jnp.abs(pos - block) == 1)

    def line_copy(block, chunk, direction):
        held = slot(block, half, chunk) if chunk < CHUNKS else slot(block, 1 - half, chunk - EXTRA)
        return pltpu.make_async_remote_copy(
            src_ref=held, dst_ref=held,
            send_sem=line_send.at[direction, block, chunk], recv_sem=line_recv.at[block, chunk],
            device_id=(left, right)[direction], device_id_type=MESH,
        )

    def x_copy(block, chunk, side):
        return pltpu.make_async_remote_copy(
            src_ref=slot(block, side, chunk), dst_ref=slot(block, side, chunk),
            send_sem=x_send.at[block, chunk], recv_sem=x_recv.at[block, chunk],
            device_id=across, device_id_type=MESH,
        )

    def lat_copy(source, group, owner, target, index):
        return pltpu.make_async_remote_copy(
            src_ref=source, dst_ref=lat.at[group, owner],
            send_sem=lat_send.at[index], recv_sem=lat_recv.at[index],
            device_id=target, device_id_type=MESH,
        )

    barrier = pltpu.get_barrier_semaphore()
    for target in (pair, sibling, across):
        pl.semaphore_signal(barrier, inc=1, device_id=target, device_id_type=MESH)

    @pl.when(has_left)
    def _():
        pl.semaphore_signal(barrier, inc=1, device_id=left, device_id_type=MESH)

    @pl.when(has_right)
    def _():
        pl.semaphore_signal(barrier, inc=1, device_id=right, device_id_type=MESH)

    own_lat = pltpu.make_async_copy(latents, turned_lat, own_sem.at[0])
    own = []
    for h in range(nh):
        j, a = h // 2, h % 2
        for start, size, at in (
            (0, nope, a * nope), (nope, r, 2 * nope + a * r), (nope + r, r, 2 * nope + 2 * r + a * r)
        ):
            own.append((wq.at[pl.ds(h * head + start, size), :], wq_buf.at[pos, pl.ds(2 * j * head + at, size), :]))
    for side in range(2):
        own.append((wkv.at[:, pl.ds(side * per * width, per * width)], wkv_buf.at[pos, side]))
    own = [pltpu.make_async_copy(*ends, own_sem.at[1 + i]) for i, ends in enumerate(own)]
    own_lat.start()
    for copy in own:
        copy.start()

    pl.semaphore_wait(barrier, 3 + has_left.astype(jnp.int32) + has_right.astype(jnp.int32))

    for copy in own:
        copy.wait()

    @pl.when(has_left)
    def _():
        for chunk in range(CHUNKS):
            line_copy(pos, chunk, 0).start()

        @pl.when(at_end(pos))
        def _():
            for chunk in range(CHUNKS, CHUNKS + EXTRA):
                line_copy(pos, chunk, 0).start()

    @pl.when(has_right)
    def _():
        for chunk in range(CHUNKS):
            line_copy(pos, chunk, 1).start()

        @pl.when(at_end(pos))
        def _():
            for chunk in range(CHUNKS, CHUNKS + EXTRA):
                line_copy(pos, chunk, 1).start()

    def pass_on(block, chunk, direction):
        line_copy(block, chunk, 1 - direction).wait_recv()

        @pl.when((has_left, has_right)[direction])
        def _():
            line_copy(block, chunk, direction).start()

        if chunk < CHUNKS - EXTRA:
            x_copy(block, chunk, half).start()
        else:

            @pl.when(jnp.logical_not(direct(block)))
            def _():
                x_copy(block, chunk, half).start()

    def forward(distance, chunk):
        def both(condition, block, direction):
            @pl.when(condition)
            def _():
                pass_on(block, chunk, direction)

        both(pos - distance >= 0, jnp.maximum(pos - distance, 0), 1)
        both(pos + distance < n_line, jnp.minimum(pos + distance, n_line - 1), 0)

    unit = tokens // slots

    def tables(group):
        index = jnp.where(group == 0, seq, seq + 1 - 2 * parity)
        spans = []
        begin = jnp.int32(0)
        for i in range(slots):
            end = begin + lengths[index, i]
            spans.append((begin, end))
            begin = end

        def begins_of(ids):
            found = jnp.zeros_like(ids)
            for low, high in spans:
                found = jnp.where((ids >= low) & (ids < high), low, found)
            return found

        freq = freqs[...]
        fine = lax.broadcasted_iota(jnp.int32, (unit, 128), 0).astype(jnp.float32) * freq
        fine_cos, fine_sin = jnp.cos(fine), jnp.sin(fine)
        coarse_ids = lax.broadcasted_iota(jnp.int32, (slots, 128), 0) * unit
        coarse = (coarse_ids - begins_of(coarse_ids)).astype(jnp.float32) * freq
        coarse_cos, coarse_sin = jnp.cos(coarse), jnp.sin(coarse)
        lanes = lax.broadcasted_iota(jnp.int32, (unit, 128), 1)
        sign = jnp.where(lanes < 64, -1.0, 1.0).astype(jnp.float32)
        for i in range(slots):
            c, s = coarse_cos[i : i + 1], coarse_sin[i : i + 1]
            cosine[group, pl.ds(i * unit, unit), :] = fine_cos * c - fine_sin * s
            sine[group, pl.ds(i * unit, unit), :] = (fine_sin * c + fine_cos * s) * sign
        for i in range(slots):
            rows = lax.broadcasted_iota(jnp.int32, (unit, tokens), 0) + i * unit
            cols = lax.broadcasted_iota(jnp.int32, (unit, tokens), 1)
            first = begins_of(jnp.full((1, tokens), i * unit, jnp.int32))
            allowed = (first <= cols) & (cols <= rows)
            bias[group, pl.ds(i * unit, unit), :] = jnp.where(allowed, 0.0, MASKED).astype(jnp.float32)

    def normalize(group, owner):
        step_rows = 64

        def step(i, carry):
            source = pl.ds(pl.multiple_of(i * step_rows, step_rows), step_rows)
            target = pl.ds(pl.multiple_of(owner * half_tokens + i * step_rows, step_rows), step_rows)
            q_part = lat[group, owner, source, 0:q_width].astype(jnp.float32)
            squares = jnp.mean(q_part * q_part, axis=-1, keepdims=True)
            qn[group, target, :] = (q_part * lax.rsqrt(squares + EPSILON) * gains[0:1, 0:q_width]).astype(jnp.bfloat16)
            kv_part = lat[group, owner, source, q_width : q_width + kv_width].astype(jnp.float32)
            squares = jnp.mean(kv_part * kv_part, axis=-1, keepdims=True)
            kvn[group, target, :] = (kv_part * lax.rsqrt(squares + EPSILON) * gains[0:1, q_width : q_width + kv_width]).astype(jnp.bfloat16)
            tail = lat[group, owner, source, q_width + kv_width :].astype(jnp.float32)
            tail = jnp.concatenate([tail, tail], axis=1)
            lanes = lax.broadcasted_iota(jnp.int32, tail.shape, 1)
            tail = jnp.where((lanes >= r) & (lanes < 3 * r), pltpu.roll(tail, r, 1), tail)
            turned = tail * cosine[group, target, :] + pltpu.roll(tail, 64, 1) * sine[group, target, :]
            first = lax.rem(lanes, 64) < 32
            kr[group, 0, target, :] = jnp.where(first, turned, 0.0).astype(jnp.bfloat16)
            kr[group, 1, target, :] = jnp.where(first, 0.0, turned).astype(jnp.bfloat16)
            return carry

        lax.fori_loop(0, half_tokens // step_rows, step, 0)

    factor = (nope + rope) ** (-0.5) * math.log2(math.e)
    tile = tokens // 2

    def attend(block, group, j):
        q_at = pl.ds(pl.multiple_of(j * 2 * head, 2 * head), 2 * head)
        for i in range(2):
            rows = pl.ds(i * tile, tile)
            q = lax.dot_general(
                qn[group, rows, :], wq_buf[block, q_at, :], (((1,), (1,)), ((), ())),
                preferred_element_type=jnp.float32,
            )
            tail = q[:, 2 * nope :]
            turned = tail * cosine[group, rows, :] + pltpu.roll(tail, 64, 1) * sine[group, rows, :]
            turned = turned.astype(jnp.bfloat16)
            for a in range(2):
                q_s[a, rows, 0:nope] = q[:, a * nope : (a + 1) * nope].astype(jnp.bfloat16)
                q_s[a, rows, nope:] = turned
                if split:
                    side, at = j // (per // 2), lax.rem(j, per // 2) * 2 + a
                else:
                    side, at = (2 * j + a) // per, lax.rem(2 * j + a, per)
                if per <= 2:
                    at = a if split else 0
                    kv_at = pl.ds(at * width, width)
                else:
                    kv_at = pl.ds(pl.multiple_of(at * width, width), width)
                kv = jnp.dot(
                    kvn[group, rows, :], wkv_buf[block, side, :, kv_at],
                    preferred_element_type=jnp.float32,
                ).astype(jnp.bfloat16)
                k_s[a, rows, 0:nope] = kv[:, 0:nope]
                k_s[a, rows, nope:] = kr[group, a, rows, :]
                v_s[a, rows, :] = kv[:, nope:]
        for a in range(2):
            for i in range(2):
                rows = pl.ds(i * tile, tile)
                span = (i + 1) * tile
                scores = lax.dot_general(
                    q_s[a, rows, :], k_s[a, 0:span, :], (((1,), (1,)), ((), ())),
                    preferred_element_type=jnp.float32,
                )
                scores = scores + bias[group, rows, 0:span]
                top = jnp.max(scores, axis=-1, keepdims=True)
                terms = jnp.exp2((scores - top) * factor)
                total = jnp.sum(terms, axis=-1, keepdims=True)
                mixed = jnp.dot(
                    terms.astype(jnp.bfloat16), v_s[a, 0:span, :], preferred_element_type=jnp.float32
                )
                mixed = (mixed / total).astype(jnp.bfloat16)
                at = pl.multiple_of(((2 * block + parity) * per + j) * 2 * vd + a * vd, vd)

                @pl.when(group == 0)
                def _():
                    out[rows, pl.ds(at, vd)] = mixed

                @pl.when(group == 1)
                def _():
                    obuf[block, j, rows, a * vd : (a + 1) * vd] = mixed

    def columns(owner, block, j):
        return pl.ds(pl.multiple_of(((2 * block + owner) * per + j) * 2 * vd, 2 * vd), 2 * vd)

    def pair_out(block, j, owner):
        return pltpu.make_async_remote_copy(
            src_ref=obuf.at[block, j], dst_ref=out.at[:, columns(owner, block, j)],
            send_sem=out_send.at[block, j], recv_sem=out_recv.at[block, j],
            device_id=pair, device_id_type=MESH,
        )

    own_lat.wait()
    wide = turned_lat.shape[0]
    for low in range(0, wide, 128):
        high = min(low + 128, wide)
        lat[0, core, :, low:high] = turned_lat[low:high, :].T
    gains[0:1, 0:q_width] = q_gain[...].reshape(1, q_width)
    gains[0:1, q_width:] = kv_gain[...].reshape(1, kv_width)
    lax.fori_loop(0, 2, lambda g, c: (tables(g), c)[1], 0)
    lat_copy(lat.at[0, core], 0, core, sibling, 0).start()
    lat_copy(lat.at[0, core], 1, core, pair, 1).start()
    normalize(0, core)
    lat_copy(lat.at[0, core], 0, 1 - core, sibling, 0).wait_recv()
    normalize(0, 1 - core)
    forward(1, 0)

    def own_step(u, carry):
        g, j = u // per, lax.rem(u, per)

        @pl.when(u == per)
        def _():
            forward(1, 2)
            lat_copy(lat.at[0, core], 1, core, pair, 1).wait_recv()
            lat_copy(lat.at[1, core], 1, core, sibling, 2).start()
            forward(1, 3)
            normalize(1, core)
            lat_copy(lat.at[1, 1 - core], 1, 1 - core, sibling, 2).wait_recv()
            normalize(1, 1 - core)
            forward(1, 4)

        attend(pos, g, j)

        @pl.when(u == 0)
        def _():
            forward(1, 1)

        @pl.when(g == 1)
        def _():
            pair_out(pos, j, parity).start()

        return carry

    lax.fori_loop(0, 2 * per, own_step, 0)
    forward(1, 5)

    def work(t, first, count, wait):
        def side(n, inner):
            block = pos + (2 * n - 1) * t

            @pl.when((block >= 0) & (block < n_line))
            def _():
                held = jnp.clip(block, 0, n_line - 1)

                @pl.when(wait)
                def _():
                    for chunk in range(CHUNKS - EXTRA):
                        x_copy(held, chunk, 1 - half).wait_recv()

                    @pl.when(direct(held))
                    def _():
                        for chunk in range(CHUNKS, CHUNKS + EXTRA):
                            line_copy(held, chunk, 0).wait_recv()

                    @pl.when(jnp.logical_not(direct(held)))
                    def _():
                        for chunk in range(CHUNKS - EXTRA, CHUNKS):
                            x_copy(held, chunk, 1 - half).wait_recv()

                def unit_step(i, rest):
                    j, g = first + i // 2, 1 - lax.rem(i, 2)
                    attend(held, g, j)

                    @pl.when(g == 1)
                    def _():
                        pair_out(held, j, parity).start()

                    return rest

                lax.fori_loop(0, 2 * count, unit_step, 0)

            return inner

        lax.fori_loop(0, 2, side, 0)

    def stage(i, carry):
        t, late = i // 2, lax.rem(i, 2) == 0

        @pl.when(late & (t < n_line))
        def _():
            for chunk in range(CHUNKS // 2):
                forward(t, chunk)

        outer = jnp.logical_not(has_left & has_right)

        def rest_of(t):
            for chunk in range(CHUNKS // 2, CHUNKS):
                forward(t, chunk)

        @pl.when(late & (t < n_line) & jnp.logical_not(outer))
        def _():
            rest_of(t)

        if split:
            count = per // 2
            first = jnp.where(late, 1 - half, half) * count
            work(jnp.where(late, t - 1, t), first, count, late)
        else:

            @pl.when(late)
            def _():
                work(t - 1, 0, per, late)

        @pl.when(late & (t < n_line) & outer)
        def _():
            rest_of(t)

        return carry

    lax.fori_loop(4 - int(split), 2 * n_line + 1, stage, 0)

    lat_copy(lat.at[0, core], 0, core, sibling, 0).wait_send()
    lat_copy(lat.at[0, core], 1, core, pair, 1).wait_send()
    lat_copy(lat.at[1, core], 1, core, sibling, 2).wait_send()

    def drain(block, carry):
        for goes, direction in (((block <= pos) & has_right, 1), ((block >= pos) & has_left, 0)):

            @pl.when(goes)
            def _():
                for chunk in range(CHUNKS):
                    line_copy(block, chunk, direction).wait_send()

                @pl.when(at_end(block) & (block == pos))
                def _():
                    for chunk in range(CHUNKS, CHUNKS + EXTRA):
                        line_copy(block, chunk, direction).wait_send()

        @pl.when(block != pos)
        def _():
            for chunk in range(CHUNKS - EXTRA):
                x_copy(block, chunk, half).wait_send()

            @pl.when(jnp.logical_not(direct(block)))
            def _():
                for chunk in range(CHUNKS - EXTRA, CHUNKS):
                    x_copy(block, chunk, half).wait_send()

        for j in range(per):
            pair_out(block, j, parity).wait_send()
            pair_out(block, j, 1 - parity).wait_recv()
        return carry

    lax.fori_loop(0, n_line, drain, 0)


def shards(latents, q_gain, kv_gain, q_weight, kv_weight, lengths):
    q_width, kv_width = q_gain.shape[0], kv_gain.shape[0]
    rope = latents.shape[1] - q_width - kv_width
    nh = q_weight.shape[2]
    nope = q_weight.shape[3] - rope
    vd = kv_weight.shape[3] - nope
    n_seq = lax.axis_size("seq")
    n_line = n_seq // 2
    half_tokens = latents.shape[0]
    tokens = half_tokens * lax.axis_size("head")
    slots = lengths.shape[1]
    r = rope // 2

    wide = latents.shape[1]
    wq = jnp.transpose(q_weight[0], (1, 2, 0)).reshape(nh * (nope + rope), q_width)
    wkv = kv_weight[0].reshape(kv_width, nh * (nope + vd))
    base = 10000.0 ** (-2.0 * np.arange(r) / rope)
    freqs = jnp.asarray(np.tile(base, 4)[None, :], jnp.float32)

    vmem = pl.BlockSpec(memory_space=pltpu.VMEM)
    hbm = pl.BlockSpec(memory_space=pl.ANY)
    bf16, f32, dma = jnp.bfloat16, jnp.float32, pltpu.SemaphoreType.DMA
    heads_total = nh * n_seq
    return pl.pallas_call(
        functools.partial(kernel, n_line, nh, q_width, kv_width, rope, nope, vd, tokens, slots),
        out_shape=pltpu.VMEM((tokens, heads_total * vd), bf16),
        in_specs=[pl.BlockSpec(memory_space=pltpu.SMEM), vmem, vmem, vmem, hbm, hbm, hbm],
        out_specs=vmem,
        scratch_shapes=[
            pltpu.VMEM((n_line,) + wq.shape, bf16),
            pltpu.VMEM((n_line, 2, kv_width, nh * (nope + vd) // 2), bf16),
            pltpu.VMEM((2, 2, half_tokens, wide), bf16),
            pltpu.VMEM((2, tokens, q_width), bf16),
            pltpu.VMEM((2, tokens, kv_width), bf16),
            pltpu.VMEM((2, tokens, 128), f32),
            pltpu.VMEM((2, tokens, 128), f32),
            pltpu.VMEM((2, 2, tokens, 128), bf16),
            pltpu.VMEM((2, tokens, tokens), f32),
            pltpu.VMEM((2, tokens, nope + 128), bf16),
            pltpu.VMEM((2, tokens, nope + 128), bf16),
            pltpu.VMEM((2, tokens, vd), bf16),
            pltpu.VMEM((n_line, nh // 2, tokens, 2 * vd), bf16),
            pltpu.VMEM((8, q_width + kv_width), f32),
            pltpu.VMEM((wide, half_tokens), bf16),
            dma((3 * nh + 3,)), dma((3,)), dma((3,)),
            dma((2, n_line, CHUNKS + EXTRA)), dma((n_line, CHUNKS + EXTRA)),
            dma((n_line, CHUNKS)), dma((n_line, CHUNKS)),
            dma((n_line, nh // 2)), dma((n_line, nh // 2)),
        ],
        compiler_params=pltpu.CompilerParams(
            collective_id=0, has_side_effects=True, vmem_limit_bytes=59 * 1024 * 1024
        ),
    )(lengths, freqs, q_gain, kv_gain, latents.T, wq, wkv)


def solution(mesh):
    return jax.shard_map(
        shards,
        mesh=mesh,
        in_specs=(
            P(("parts", "seq", "head"), None),
            P(),
            P(),
            P("head", None, "seq", None),
            P("head", None, "seq", None),
            P("parts", None),
        ),
        out_specs=P(("parts", "seq"), "head"),
        check_vma=False,
    )
```

```python
import functools
import math

import jax
import jax.numpy as jnp
import numpy as np
from jax import lax
from jax.experimental import pallas as pl
from jax.experimental.pallas import tpu as pltpu
from jax.sharding import PartitionSpec as P

EPSILON = 1e-06
MASKED = -1e30
CHUNKS = 8
EXTRA = 4
MESH = pl.DeviceIdType.MESH


def kernel(
    n_line, nh, q_width, kv_width, rope, nope, vd, tokens, slots,
    lengths, freqs, q_gain, kv_gain, latents, wq, wkv,
    out,
    wq_buf, wkv_buf, lat, qn, kvn, cosine, sine, kr, bias, q_s, k_s, v_s, obuf, gains, turned_lat,
    own_sem, lat_send, lat_recv, line_send, line_recv, x_send, x_recv, out_send, out_recv,
):
    part = lax.axis_index("parts")
    seq = lax.axis_index("seq")
    core = lax.axis_index("head")
    half = lax.rem(part, 2)
    pos = seq // 2
    parity = lax.rem(seq, 2)
    pair = {"seq": seq + 1 - 2 * parity}
    sibling = {"head": 1 - core}
    across = {"parts": part + 1 - 2 * half}
    left = {"seq": jnp.maximum(seq - 2, parity)}
    right = {"seq": jnp.minimum(seq + 2, 2 * (n_line - 1) + parity)}
    has_left = pos > 0
    has_right = pos < n_line - 1
    half_tokens = tokens // 2
    per = nh // 2
    split = per % 2 == 0
    head = nope + rope
    width = nope + vd
    r = rope // 2
    q_rows = nh * head // 8
    kv_rows = kv_width // 4

    def slot(block, side, chunk):
        if 2 <= chunk < 6:
            start = pl.multiple_of(side * (4 * q_rows) + (chunk - 2) * q_rows, q_rows)
            return wq_buf.at[block, pl.ds(start, q_rows), :]
        return wkv_buf.at[block, side, pl.ds((chunk if chunk < 2 else chunk - 4) * kv_rows, kv_rows), :]

    def at_end(block):
        return (block == 0) | (block == n_line - 1)

    def direct(block):
        return at_end(block) & (jnp.abs(pos - block) == 1)

    def line_copy(block, chunk, direction):
        held = slot(block, half, chunk) if chunk < CHUNKS else slot(block, 1 - half, chunk - EXTRA)
        return pltpu.make_async_remote_copy(
            src_ref=held, dst_ref=held,
            send_sem=line_send.at[direction, block, chunk], recv_sem=line_recv.at[block, chunk],
            device_id=(left, right)[direction], device_id_type=MESH,
        )

    def x_copy(block, chunk, side):
        return pltpu.make_async_remote_copy(
            src_ref=slot(block, side, chunk), dst_ref=slot(block, side, chunk),
            send_sem=x_send.at[block, chunk], recv_sem=x_recv.at[block, chunk],
            device_id=across, device_id_type=MESH,
        )

    def lat_copy(source, group, owner, target, index):
        return pltpu.make_async_remote_copy(
            src_ref=source, dst_ref=lat.at[group, owner],
            send_sem=lat_send.at[index], recv_sem=lat_recv.at[index],
            device_id=target, device_id_type=MESH,
        )

    barrier = pltpu.get_barrier_semaphore()
    for target in (pair, sibling, across):
        pl.semaphore_signal(barrier, inc=1, device_id=target, device_id_type=MESH)

    @pl.when(has_left)
    def _():
        pl.semaphore_signal(barrier, inc=1, device_id=left, device_id_type=MESH)

    @pl.when(has_right)
    def _():
        pl.semaphore_signal(barrier, inc=1, device_id=right, device_id_type=MESH)

    own_lat = pltpu.make_async_copy(latents, turned_lat, own_sem.at[0])
    own = []
    for h in range(nh):
        j, a = h // 2, h % 2
        for start, size, at in (
            (0, nope, a * nope), (nope, r, 2 * nope + a * r), (nope + r, r, 2 * nope + 2 * r + a * r)
        ):
            own.append((wq.at[pl.ds(h * head + start, size), :], wq_buf.at[pos, pl.ds(2 * j * head + at, size), :]))
    for side in range(2):
        own.append((wkv.at[:, pl.ds(side * per * width, per * width)], wkv_buf.at[pos, side]))
    own = [pltpu.make_async_copy(*ends, own_sem.at[1 + i]) for i, ends in enumerate(own)]
    own_lat.start()
    for copy in own:
        copy.start()

    pl.semaphore_wait(barrier, 3 + has_left.astype(jnp.int32) + has_right.astype(jnp.int32))

    for copy in own:
        copy.wait()

    @pl.when(has_left)
    def _():
        for chunk in range(CHUNKS):
            line_copy(pos, chunk, 0).start()

        @pl.when(at_end(pos))
        def _():
            for chunk in range(CHUNKS, CHUNKS + EXTRA):
                line_copy(pos, chunk, 0).start()

    @pl.when(has_right)
    def _():
        for chunk in range(CHUNKS):
            line_copy(pos, chunk, 1).start()

        @pl.when(at_end(pos))
        def _():
            for chunk in range(CHUNKS, CHUNKS + EXTRA):
                line_copy(pos, chunk, 1).start()

    def pass_on(block, chunk, direction):
        line_copy(block, chunk, 1 - direction).wait_recv()

        @pl.when((has_left, has_right)[direction])
        def _():
            line_copy(block, chunk, direction).start()

        if chunk < CHUNKS - EXTRA:
            x_copy(block, chunk, half).start()
        else:

            @pl.when(jnp.logical_not(direct(block)))
            def _():
                x_copy(block, chunk, half).start()

    def forward(distance, chunk):
        def both(condition, block, direction):
            @pl.when(condition)
            def _():
                pass_on(block, chunk, direction)

        both(pos - distance >= 0, jnp.maximum(pos - distance, 0), 1)
        both(pos + distance < n_line, jnp.minimum(pos + distance, n_line - 1), 0)

    unit = tokens // slots

    def tables(group):
        index = jnp.where(group == 0, seq, seq + 1 - 2 * parity)
        spans = []
        begin = jnp.int32(0)
        for i in range(slots):
            end = begin + lengths[index, i]
            spans.append((begin, end))
            begin = end

        def begins_of(ids):
            found = jnp.zeros_like(ids)
            for low, high in spans:
                found = jnp.where((ids >= low) & (ids < high), low, found)
            return found

        freq = freqs[...]
        fine = lax.broadcasted_iota(jnp.int32, (unit, 128), 0).astype(jnp.float32) * freq
        fine_cos, fine_sin = jnp.cos(fine), jnp.sin(fine)
        coarse_ids = lax.broadcasted_iota(jnp.int32, (slots, 128), 0) * unit
        coarse = (coarse_ids - begins_of(coarse_ids)).astype(jnp.float32) * freq
        coarse_cos, coarse_sin = jnp.cos(coarse), jnp.sin(coarse)
        lanes = lax.broadcasted_iota(jnp.int32, (unit, 128), 1)
        sign = jnp.where(lanes < 64, -1.0, 1.0).astype(jnp.float32)
        for i in range(slots):
            c, s = coarse_cos[i : i + 1], coarse_sin[i : i + 1]
            cosine[group, pl.ds(i * unit, unit), :] = fine_cos * c - fine_sin * s
            sine[group, pl.ds(i * unit, unit), :] = (fine_sin * c + fine_cos * s) * sign
        for i in range(slots):
            rows = lax.broadcasted_iota(jnp.int32, (unit, tokens), 0) + i * unit
            cols = lax.broadcasted_iota(jnp.int32, (unit, tokens), 1)
            first = begins_of(jnp.full((1, tokens), i * unit, jnp.int32))
            allowed = (first <= cols) & (cols <= rows)
            bias[group, pl.ds(i * unit, unit), :] = jnp.where(allowed, 0.0, MASKED).astype(jnp.float32)

    def normalize(group, owner):
        step_rows = 64

        def step(i, carry):
            source = pl.ds(pl.multiple_of(i * step_rows, step_rows), step_rows)
            target = pl.ds(pl.multiple_of(owner * half_tokens + i * step_rows, step_rows), step_rows)
            q_part = lat[group, owner, source, 0:q_width].astype(jnp.float32)
            squares = jnp.mean(q_part * q_part, axis=-1, keepdims=True)
            qn[group, target, :] = (q_part * lax.rsqrt(squares + EPSILON) * gains[0:1, 0:q_width]).astype(jnp.bfloat16)
            kv_part = lat[group, owner, source, q_width : q_width + kv_width].astype(jnp.float32)
            squares = jnp.mean(kv_part * kv_part, axis=-1, keepdims=True)
            kvn[group, target, :] = (kv_part * lax.rsqrt(squares + EPSILON) * gains[0:1, q_width : q_width + kv_width]).astype(jnp.bfloat16)
            tail = lat[group, owner, source, q_width + kv_width :].astype(jnp.float32)
            tail = jnp.concatenate([tail, tail], axis=1)
            lanes = lax.broadcasted_iota(jnp.int32, tail.shape, 1)
            tail = jnp.where((lanes >= r) & (lanes < 3 * r), pltpu.roll(tail, r, 1), tail)
            turned = tail * cosine[group, target, :] + pltpu.roll(tail, 64, 1) * sine[group, target, :]
            first = lax.rem(lanes, 64) < 32
            kr[group, 0, target, :] = jnp.where(first, turned, 0.0).astype(jnp.bfloat16)
            kr[group, 1, target, :] = jnp.where(first, 0.0, turned).astype(jnp.bfloat16)
            return carry

        lax.fori_loop(0, half_tokens // step_rows, step, 0)

    factor = (nope + rope) ** (-0.5) * math.log2(math.e)
    tile = tokens // 2

    def attend(block, group, j):
        q_at = pl.ds(pl.multiple_of(j * 2 * head, 2 * head), 2 * head)
        for i in range(2):
            rows = pl.ds(i * tile, tile)
            q = lax.dot_general(
                qn[group, rows, :], wq_buf[block, q_at, :], (((1,), (1,)), ((), ())),
                preferred_element_type=jnp.float32,
            )
            tail = q[:, 2 * nope :]
            turned = tail * cosine[group, rows, :] + pltpu.roll(tail, 64, 1) * sine[group, rows, :]
            turned = turned.astype(jnp.bfloat16)
            for a in range(2):
                q_s[a, rows, 0:nope] = q[:, a * nope : (a + 1) * nope].astype(jnp.bfloat16)
                q_s[a, rows, nope:] = turned
                if split:
                    side, at = j // (per // 2), lax.rem(j, per // 2) * 2 + a
                else:
                    side, at = (2 * j + a) // per, lax.rem(2 * j + a, per)
                if per <= 2:
                    at = a if split else 0
                    kv_at = pl.ds(at * width, width)
                else:
                    kv_at = pl.ds(pl.multiple_of(at * width, width), width)
                kv = jnp.dot(
                    kvn[group, rows, :], wkv_buf[block, side, :, kv_at],
                    preferred_element_type=jnp.float32,
                ).astype(jnp.bfloat16)
                k_s[a, rows, 0:nope] = kv[:, 0:nope]
                k_s[a, rows, nope:] = kr[group, a, rows, :]
                v_s[a, rows, :] = kv[:, nope:]
        for a in range(2):
            for i in range(2):
                rows = pl.ds(i * tile, tile)
                span = (i + 1) * tile
                scores = lax.dot_general(
                    q_s[a, rows, :], k_s[a, 0:span, :], (((1,), (1,)), ((), ())),
                    preferred_element_type=jnp.float32,
                )
                scores = scores + bias[group, rows, 0:span]
                top = jnp.max(scores, axis=-1, keepdims=True)
                terms = jnp.exp2((scores - top) * factor)
                total = jnp.sum(terms, axis=-1, keepdims=True)
                mixed = jnp.dot(
                    terms.astype(jnp.bfloat16), v_s[a, 0:span, :], preferred_element_type=jnp.float32
                )
                mixed = (mixed / total).astype(jnp.bfloat16)
                at = pl.multiple_of(((2 * block + parity) * per + j) * 2 * vd + a * vd, vd)

                @pl.when(group == 0)
                def _():
                    out[rows, pl.ds(at, vd)] = mixed

                @pl.when(group == 1)
                def _():
                    obuf[block, j, rows, a * vd : (a + 1) * vd] = mixed

    def columns(owner, block, j):
        return pl.ds(pl.multiple_of(((2 * block + owner) * per + j) * 2 * vd, 2 * vd), 2 * vd)

    def pair_out(block, j, owner):
        return pltpu.make_async_remote_copy(
            src_ref=obuf.at[block, j], dst_ref=out.at[:, columns(owner, block, j)],
            send_sem=out_send.at[block, j], recv_sem=out_recv.at[block, j],
            device_id=pair, device_id_type=MESH,
        )

    own_lat.wait()
    wide = turned_lat.shape[0]
    for low in range(0, wide, 128):
        high = min(low + 128, wide)
        lat[0, core, :, low:high] = turned_lat[low:high, :].T
    gains[0:1, 0:q_width] = q_gain[...].reshape(1, q_width)
    gains[0:1, q_width:] = kv_gain[...].reshape(1, kv_width)
    lax.fori_loop(0, 2, lambda g, c: (tables(g), c)[1], 0)
    lat_copy(lat.at[0, core], 0, core, sibling, 0).start()
    lat_copy(lat.at[0, core], 1, core, pair, 1).start()
    forward(1, 0)
    normalize(0, core)
    forward(1, 1)
    lat_copy(lat.at[0, core], 0, 1 - core, sibling, 0).wait_recv()
    normalize(0, 1 - core)

    def own_step(u, carry):
        g, j = u // per, lax.rem(u, per)

        @pl.when(u == per)
        def _():
            forward(1, 3)
            lat_copy(lat.at[0, core], 1, core, pair, 1).wait_recv()
            lat_copy(lat.at[1, core], 1, core, sibling, 2).start()
            forward(1, 4)
            normalize(1, core)
            lat_copy(lat.at[1, 1 - core], 1, 1 - core, sibling, 2).wait_recv()
            normalize(1, 1 - core)
            forward(1, 5)

        attend(pos, g, j)

        @pl.when(u == 0)
        def _():
            forward(1, 2)

        @pl.when(g == 1)
        def _():
            pair_out(pos, j, parity).start()

        return carry

    lax.fori_loop(0, 2 * per, own_step, 0)
    forward(1, 6)
    forward(1, 7)

    def work(t, first, count, wait):
        def side(n, inner):
            block = pos + (2 * n - 1) * t

            @pl.when((block >= 0) & (block < n_line))
            def _():
                held = jnp.clip(block, 0, n_line - 1)

                @pl.when(wait)
                def _():
                    for chunk in range(CHUNKS - EXTRA):
                        x_copy(held, chunk, 1 - half).wait_recv()

                    @pl.when(direct(held))
                    def _():
                        for chunk in range(CHUNKS, CHUNKS + EXTRA):
                            line_copy(held, chunk, 0).wait_recv()

                    @pl.when(jnp.logical_not(direct(held)))
                    def _():
                        for chunk in range(CHUNKS - EXTRA, CHUNKS):
                            x_copy(held, chunk, 1 - half).wait_recv()

                def unit_step(i, rest):
                    j, g = first + i // 2, 1 - lax.rem(i, 2)
                    attend(held, g, j)

                    @pl.when(g == 1)
                    def _():
                        pair_out(held, j, parity).start()

                    return rest

                lax.fori_loop(0, 2 * count, unit_step, 0)

            return inner

        lax.fori_loop(0, 2, side, 0)

    def stage(i, carry):
        t, late = i // 2, lax.rem(i, 2) == 0

        @pl.when(late & (t < n_line))
        def _():
            for chunk in range(CHUNKS // 2):
                forward(t, chunk)

        outer = jnp.logical_not(has_left & has_right)

        def rest_of(t):
            for chunk in range(CHUNKS // 2, CHUNKS):
                forward(t, chunk)

        @pl.when(late & (t < n_line) & jnp.logical_not(outer))
        def _():
            rest_of(t)

        if split:
            count = per // 2
            first = jnp.where(late, 1 - half, half) * count
            work(jnp.where(late, t - 1, t), first, count, late)
        else:

            @pl.when(late)
            def _():
                work(t - 1, 0, per, late)

        @pl.when(late & (t < n_line) & outer)
        def _():
            rest_of(t)

        return carry

    lax.fori_loop(4 - int(split), 2 * n_line + 1, stage, 0)

    lat_copy(lat.at[0, core], 0, core, sibling, 0).wait_send()
    lat_copy(lat.at[0, core], 1, core, pair, 1).wait_send()
    lat_copy(lat.at[1, core], 1, core, sibling, 2).wait_send()

    def drain(block, carry):
        for goes, direction in (((block <= pos) & has_right, 1), ((block >= pos) & has_left, 0)):

            @pl.when(goes)
            def _():
                for chunk in range(CHUNKS):
                    line_copy(block, chunk, direction).wait_send()

                @pl.when(at_end(block) & (block == pos))
                def _():
                    for chunk in range(CHUNKS, CHUNKS + EXTRA):
                        line_copy(block, chunk, direction).wait_send()

        @pl.when(block != pos)
        def _():
            for chunk in range(CHUNKS - EXTRA):
                x_copy(block, chunk, half).wait_send()

            @pl.when(jnp.logical_not(direct(block)))
            def _():
                for chunk in range(CHUNKS - EXTRA, CHUNKS):
                    x_copy(block, chunk, half).wait_send()

        for j in range(per):
            pair_out(block, j, parity).wait_send()
            pair_out(block, j, 1 - parity).wait_recv()
        return carry

    lax.fori_loop(0, n_line, drain, 0)


def shards(latents, q_gain, kv_gain, q_weight, kv_weight, lengths):
    q_width, kv_width = q_gain.shape[0], kv_gain.shape[0]
    rope = latents.shape[1] - q_width - kv_width
    nh = q_weight.shape[2]
    nope = q_weight.shape[3] - rope
    vd = kv_weight.shape[3] - nope
    n_seq = lax.axis_size("seq")
    n_line = n_seq // 2
    half_tokens = latents.shape[0]
    tokens = half_tokens * lax.axis_size("head")
    slots = lengths.shape[1]
    r = rope // 2

    wide = latents.shape[1]
    wq = jnp.transpose(q_weight[0], (1, 2, 0)).reshape(nh * (nope + rope), q_width)
    wkv = kv_weight[0].reshape(kv_width, nh * (nope + vd))
    base = 10000.0 ** (-2.0 * np.arange(r) / rope)
    freqs = jnp.asarray(np.tile(base, 4)[None, :], jnp.float32)

    vmem = pl.BlockSpec(memory_space=pltpu.VMEM)
    hbm = pl.BlockSpec(memory_space=pl.ANY)
    bf16, f32, dma = jnp.bfloat16, jnp.float32, pltpu.SemaphoreType.DMA
    heads_total = nh * n_seq
    return pl.pallas_call(
        functools.partial(kernel, n_line, nh, q_width, kv_width, rope, nope, vd, tokens, slots),
        out_shape=pltpu.VMEM((tokens, heads_total * vd), bf16),
        in_specs=[pl.BlockSpec(memory_space=pltpu.SMEM), vmem, vmem, vmem, hbm, hbm, hbm],
        out_specs=vmem,
        scratch_shapes=[
            pltpu.VMEM((n_line,) + wq.shape, bf16),
            pltpu.VMEM((n_line, 2, kv_width, nh * (nope + vd) // 2), bf16),
            pltpu.VMEM((2, 2, half_tokens, wide), bf16),
            pltpu.VMEM((2, tokens, q_width), bf16),
            pltpu.VMEM((2, tokens, kv_width), bf16),
            pltpu.VMEM((2, tokens, 128), f32),
            pltpu.VMEM((2, tokens, 128), f32),
            pltpu.VMEM((2, 2, tokens, 128), bf16),
            pltpu.VMEM((2, tokens, tokens), f32),
            pltpu.VMEM((2, tokens, nope + 128), bf16),
            pltpu.VMEM((2, tokens, nope + 128), bf16),
            pltpu.VMEM((2, tokens, vd), bf16),
            pltpu.VMEM((n_line, nh // 2, tokens, 2 * vd), bf16),
            pltpu.VMEM((8, q_width + kv_width), f32),
            pltpu.VMEM((wide, half_tokens), bf16),
            dma((3 * nh + 3,)), dma((3,)), dma((3,)),
            dma((2, n_line, CHUNKS + EXTRA)), dma((n_line, CHUNKS + EXTRA)),
            dma((n_line, CHUNKS)), dma((n_line, CHUNKS)),
            dma((n_line, nh // 2)), dma((n_line, nh // 2)),
        ],
        compiler_params=pltpu.CompilerParams(
            collective_id=0, has_side_effects=True, vmem_limit_bytes=59 * 1024 * 1024
        ),
    )(lengths, freqs, q_gain, kv_gain, latents.T, wq, wkv)


def solution(mesh):
    return jax.shard_map(
        shards,
        mesh=mesh,
        in_specs=(
            P(("parts", "seq", "head"), None),
            P(),
            P(),
            P("head", None, "seq", None),
            P("head", None, "seq", None),
            P("parts", None),
        ),
        out_specs=P(("parts", "seq"), "head"),
        check_vma=False,
    )
```
